32 devices in a mesh: grp: 8 (over z, y), tm: 4 (over x, core).
Axes of the slice: x: 2, y: 2, z: 4, core: 2. Of those that a mesh axis runs over, the one named last changes fastest.
Arguments:
- voltages: bfloat16 [2, 192, 1048576], P(None, 'grp', 'tm'), may hold values from -6 to 6
- filter_taps: float32 [4, 4096], replicated, may hold values from -3 to 3
- delays: int32 [192, 1536], replicated, may hold values from 0 to 4095
- shifts: int32 [4, 512], replicated, may hold values from 0 to 2
Outputs:
- dedispersed: float32 [1536, 512, 32], P('grp', None, 'tm')
The draws below stay inside these ranges and needn't reach their ends.
All inputs are finite; a program needn't handle non-finite values.
Results may differ from the reference program's by a relative error of at most 0.0014.
Values may be sent and summed in bfloat16 or wider, within the bound.
No kernel may reach another device: no remote copies, remote signals or barrier semaphores. Data moves between devices by JAX's collectives and lax.ppermute only.
A program may use at most 192 MiB of HBM per device.

```python
import math
import jax
import jax.numpy as jnp
from jax import lax

STATIONS = 192
TRANSFORM = 4096
CHANNELS = 512
BEAMS = 1536
TAPS = 4
INTEG = 8
LEVELS = 4
SHIFT_MOST = 2
FRAMES = 256
SAMPLES = 1048576
POWER_LEN = 32


def touch_ends(result, own_key, smallest, top_value):
    longest = result.shape.index(max(result.shape))
    spots = []
    for shift in (0, 1):
        where = [jax.random.randint(jax.random.fold_in(own_key, axis), (), 0, length) for axis, length in enumerate(result.shape)]
        where[longest] = (where[longest] + shift) % result.shape[longest]
        spots.append(tuple(where))
    return result.at[spots[0]].set(smallest).at[spots[1]].set(top_value)


def level_of(own_key, dims, split, smallest, largest):
    factor_of, own = 1.0, jax.random.fold_in(own_key, 6)
    for dim, blocks in split:
        steps = jnp.exp(jax.random.uniform(jax.random.fold_in(own, dim), (blocks,), jnp.float32, smallest / len(split), largest / len(split)))
        factor_of = factor_of * jnp.repeat(steps, dims[dim] // blocks).reshape([-1 if axis == dim else 1 for axis in range(len(dims))])
    return factor_of


def noise(stream_key, dims, scale, bound, shards=(), kind=jnp.bfloat16):
    loudness = level_of(stream_key, dims, shards, -0.22, 0.18) if shards else 1.0
    entries = jax.random.normal(stream_key, dims, jnp.float32) * scale * loudness
    return jnp.minimum(jnp.maximum(entries, -bound), bound).astype(kind)


def setup_inputs(seed: int = 0) -> dict:
    arg_keys = jax.random.split(jax.random.key(seed), 5)
    return {
        "voltages": noise(arg_keys[0], (2, STATIONS, SAMPLES), 1.0, 6.0, ((1, 8), (2, 4))),
        "filter_taps": noise(arg_keys[1], (TAPS, TRANSFORM), 0.5, 3.0, (), jnp.float32),
        "delays": touch_ends(jax.random.randint(arg_keys[2], (STATIONS, BEAMS), 0, 4096), jax.random.fold_in(arg_keys[2], 1), 0, 4095).astype(jnp.int32),
        "shifts": touch_ends(jax.random.randint(arg_keys[3], (LEVELS, CHANNELS), 0, SHIFT_MOST + 1), jax.random.fold_in(arg_keys[3], 1), 0, SHIFT_MOST).astype(jnp.int32),
    }


two_pi = 2.0 * math.pi

def dft_tables():
    rows_index = jnp.arange(CHANNELS, dtype=jnp.int32)
    cols_index = jnp.arange(TRANSFORM, dtype=jnp.int32)
    product = rows_index[:, None] * cols_index[None, :] % TRANSFORM
    angles = product.astype(jnp.float32) * (two_pi / TRANSFORM)
    scaling = 1.0 / math.sqrt(TRANSFORM)
    return ((jnp.cos(angles) * scaling).astype(jnp.bfloat16), (jnp.sin(angles) * scaling).astype(jnp.bfloat16))

def beam_weights(channel, delays):
    phases = (channel * delays.T % TRANSFORM).astype(jnp.float32) * (two_pi / TRANSFORM)
    scaling = 1.0 / math.sqrt(STATIONS)
    return ((jnp.cos(phases) * scaling).astype(jnp.bfloat16), (jnp.sin(phases) * scaling).astype(jnp.bfloat16))

def dedisperse_level(leading, trailing, amounts, out_len):
    shifted = jnp.zeros(leading.shape[:3] + (2, out_len), jnp.float32)
    for offset in range(SHIFT_MOST + 1):
        selector = (amounts == offset).astype(jnp.float32)[None, :, :, :, None]
        shifted = shifted + selector * trailing[:, :, :, None, offset:offset + out_len]
    combined = 0.5 * (leading[:, :, :, None, :] + shifted)
    return combined.reshape(leading.shape[0], -1, out_len)

def reference(voltages, filter_taps, delays, shifts):
    cosine, sine = dft_tables()

    def station_spectra(station_volts):
        frames = station_volts.reshape(2, FRAMES, TRANSFORM).astype(jnp.float32)
        padded = jnp.pad(frames, ((0, 0), (TAPS - 1, 0), (0, 0)))
        filtered = jnp.zeros_like(frames)
        for tap in range(TAPS):
            start = TAPS - 1 - tap
            filtered = filtered + filter_taps[tap][None, None, :] * padded[:, start:start + FRAMES, :]
        filtered = filtered.astype(jnp.bfloat16)
        real_part = jnp.dot(cosine, filtered[0].T, preferred_element_type=jnp.float32) + jnp.dot(sine, filtered[1].T, preferred_element_type=jnp.float32)
        imag_part = jnp.dot(cosine, filtered[1].T, preferred_element_type=jnp.float32) - jnp.dot(sine, filtered[0].T, preferred_element_type=jnp.float32)
        return jnp.stack([real_part, imag_part]).astype(jnp.bfloat16)
    spectra = lax.map(station_spectra, jnp.transpose(voltages, (1, 0, 2)))

    def channel_powers(channel):
        channel_data = lax.dynamic_index_in_dim(spectra, channel, 2, keepdims=False)
        weight_cos, weight_sin = beam_weights(channel, delays)
        real_in = channel_data[:, 0, :]
        imag_in = channel_data[:, 1, :]
        beam_real = jnp.dot(weight_cos, real_in, preferred_element_type=jnp.float32) + jnp.dot(weight_sin, imag_in, preferred_element_type=jnp.float32)
        beam_imag = jnp.dot(weight_cos, imag_in, preferred_element_type=jnp.float32) - jnp.dot(weight_sin, real_in, preferred_element_type=jnp.float32)
        energy = beam_real * beam_real + beam_imag * beam_imag
        power = energy.reshape(BEAMS, POWER_LEN, INTEG).sum(axis=-1) * (1.0 / INTEG)
        return power.astype(jnp.bfloat16)
    powers = lax.map(channel_powers, jnp.arange(CHANNELS, dtype=jnp.int32))
    current = jnp.transpose(powers, (1, 0, 2)).astype(jnp.float32)
    for level_index in range(1, LEVELS + 1):
        half_width = 2 ** (level_index - 1)
        group_count = CHANNELS // (2 * half_width)
        grouped = current.reshape(BEAMS, group_count, 2, half_width, POWER_LEN)
        leading = grouped[:, :, 0]
        trailing = jnp.pad(grouped[:, :, 1], ((0, 0), (0, 0), (0, 0), (0, SHIFT_MOST)))
        amounts = shifts[level_index - 1].reshape(group_count, half_width, 2)
        current = dedisperse_level(leading, trailing, amounts, POWER_LEN)
    return current
```

```python
import functools
import math

import jax
import jax.numpy as jnp
import numpy as np
from jax import lax
from jax.experimental import pallas as pl
from jax.experimental.pallas import tpu as pltpu
from jax.sharding import PartitionSpec as P

TRANSFORM = 4096
CHANNELS = 512
TAPS = 4
INTEG = 8
LEVELS = 4
SHIFT_MOST = 2

RADIX = 4
SUB = TRANSFORM // RADIX
PER = CHANNELS // RADIX
LANES = 128
ROWS = 8
GROUP = 2**LEVELS
VMEM_LIMIT = 60 * 1024 * 1024


def shift_along(x, axis, by):
    length = lax.axis_size(axis)
    pairs = [(i, i + by) for i in range(length) if 0 <= i + by < length]
    return lax.ppermute(x, axis, pairs)


def table_factors():
    k = (RADIX * np.arange(PER)[None, :] + np.arange(RADIX)[:, None])[:, None, :]
    fine = k * np.arange(ROWS)[None, :, None] % TRANSFORM
    coarse = k * (ROWS * np.arange(SUB // ROWS))[None, :, None] % TRANSFORM
    turn = 2.0 * np.pi / TRANSFORM
    scale = 1.0 / math.sqrt(TRANSFORM)
    fine = np.stack([np.cos(fine * turn), np.sin(fine * turn)], 1)
    coarse = np.stack([np.cos(coarse * turn), np.sin(coarse * turn)], 1) * scale
    return fine.astype(np.float32), coarse.astype(np.float32)


def channel_kernel(frames, x_ref, halo_ref, taps_ref, fine_ref, coarse_ref, out_ref, table, folded, spectra, turned):
    stations = x_ref.shape[1]

    @pl.when(pl.program_id(0) == 0)
    def _():
        def build(u, carry):
            for q in range(RADIX):
                ca, sa = fine_ref[q, 0], fine_ref[q, 1]
                cs, ss = [], []
                for half in range(2):
                    cb = coarse_ref[q, 0, pl.ds(2 * u + half, 1), :]
                    sb = coarse_ref[q, 1, pl.ds(2 * u + half, 1), :]
                    cs.append(cb * ca - sb * sa)
                    ss.append(sb * ca + cb * sa)
                c = jnp.concatenate(cs, 0).astype(jnp.bfloat16)
                s = jnp.concatenate(ss, 0)
                top = pl.ds(pl.multiple_of(u * 2 * ROWS, 2 * ROWS), 2 * ROWS)
                low = pl.ds(pl.multiple_of(SUB + u * 2 * ROWS, 2 * ROWS), 2 * ROWS)
                table[q, top, :PER] = c
                table[q, top, PER:] = (-s).astype(jnp.bfloat16)
                table[q, low, :PER] = s.astype(jnp.bfloat16)
                table[q, low, PER:] = c
            return carry

        lax.fori_loop(0, SUB // (2 * ROWS), build, 0)

    def full(x):
        x = x.astype(jnp.float32)
        if stations < ROWS:
            x = jnp.concatenate([x, jnp.zeros((ROWS - stations, LANES), jnp.float32)], 0)
        return x

    parts = [(c, j) for c in range(2) for j in range(RADIX)]

    def columns(tile, carry):
        taps = [
            [
                jnp.broadcast_to(
                    taps_ref[p : p + 1, pl.ds(pl.multiple_of(j * SUB + tile * LANES, LANES), LANES)],
                    (ROWS, LANES),
                )
                for j in range(RADIX)
            ]
            for p in range(TAPS)
        ]

        def at(ref, f, c, j):
            start = pl.multiple_of(f * TRANSFORM + j * SUB + tile * LANES, LANES)
            return full(ref[c, :, pl.ds(start, LANES)])

        def filtered(f, before):
            z, after = {}, []
            for (c, j), old in zip(parts, before):
                now = at(x_ref, f, c, j)
                total = taps[0][j] * now
                for p in range(1, TAPS):
                    total = total + taps[p][j] * old[p - 1]
                z[c, j] = total
                after.append((now, *old[:-1]))
            even = [z[c, 0] + z[c, 2] for c in range(2)]
            odd = [z[c, 0] - z[c, 2] for c in range(2)]
            even1 = [z[c, 1] + z[c, 3] for c in range(2)]
            odd1 = [z[c, 1] - z[c, 3] for c in range(2)]
            y = {
                (0, 0): even[0] + even1[0], (0, 1): even[1] + even1[1],
                (2, 0): even[0] - even1[0], (2, 1): even[1] - even1[1],
                (1, 0): odd[0] + odd1[1], (1, 1): odd[1] - odd1[0],
                (3, 0): odd[0] - odd1[1], (3, 1): odd[1] + odd1[0],
            }
            return y, after

        def pair(step, before):
            f = step * 2
            first, before = filtered(f, before)
            second, before = filtered(f + 1, before)
            rows = pl.ds(pl.multiple_of(f * ROWS, 2 * ROWS), 2 * ROWS)
            for q in range(RADIX):
                for c in range(2):
                    both = jnp.concatenate([first[q, c], second[q, c]], 0)
                    lanes = pl.ds(pl.multiple_of(c * SUB + tile * LANES, LANES), LANES)
                    folded[q, rows, lanes] = both.astype(jnp.bfloat16)
            return before

        before = [tuple(at(halo_ref, TAPS - 2 - p, c, j) for p in range(TAPS - 1)) for c, j in parts]
        lax.fori_loop(0, frames // 2, pair, before)
        return carry

    lax.fori_loop(0, SUB // LANES, columns, 0)

    def residue(q, carry):
        both = jnp.dot(folded[q], table[q], preferred_element_type=jnp.float32)
        spectra[0] = both[:, :PER]
        spectra[1] = both[:, PER:]
        powers = frames // INTEG
        for s in range(stations):
            rows = [
                spectra[part, pl.ds(i * ROWS + s, powers, stride=INTEG * ROWS), :]
                for part in range(2)
                for i in range(INTEG)
            ]
            turned[pl.ds(s, PER, stride=ROWS), :] = jnp.concatenate(rows, 0).T
        block = turned[...].reshape(out_ref.shape[0], out_ref.shape[1], ROWS, LANES)
        out_ref[:, :, q] = block[:, :, :stations].astype(jnp.bfloat16)
        return carry

    lax.fori_loop(0, RADIX, residue, 0)


def channelize(voltages, halo, filter_taps, owners):
    stations = voltages.shape[1]
    frames = voltages.shape[2] // TRANSFORM
    block = ROWS if stations % ROWS == 0 else stations
    assert block <= ROWS and 2 * frames == LANES
    fine, coarse = table_factors()
    return pl.pallas_call(
        functools.partial(channel_kernel, frames),
        grid=(stations // block,),
        in_specs=[
            pl.BlockSpec((2, block, voltages.shape[2]), lambda i: (0, i, 0)),
            pl.BlockSpec((2, block, halo.shape[2]), lambda i: (0, i, 0)),
            pl.BlockSpec(filter_taps.shape, lambda i: (0, 0)),
            pl.BlockSpec(fine.shape, lambda i: (0, 0, 0, 0)),
            pl.BlockSpec(coarse.shape, lambda i: (0, 0, 0, 0)),
        ],
        out_specs=pl.BlockSpec((owners, PER // owners, RADIX, block, LANES), lambda i: (0, 0, 0, i, 0)),
        out_shape=jax.ShapeDtypeStruct((owners, PER // owners, RADIX, stations, LANES), jnp.bfloat16),
        scratch_shapes=[
            pltpu.VMEM((RADIX, 2 * SUB, 2 * PER), jnp.bfloat16),
            pltpu.VMEM((RADIX, frames * ROWS, 2 * SUB), jnp.bfloat16),
            pltpu.VMEM((2, frames * ROWS, PER), jnp.float32),
            pltpu.VMEM((PER * ROWS, LANES), jnp.float32),
        ],
        compiler_params=pltpu.CompilerParams(vmem_limit_bytes=VMEM_LIMIT),
        name="channelize",
    )(voltages, halo, filter_taps, jnp.asarray(fine), jnp.asarray(coarse))


def turn_of(steps):
    whole = 2 * TRANSFORM
    quarter = whole // 4
    moved = (steps & (whole - 1)) + quarter // 2
    x = ((moved & (quarter - 1)) - quarter // 2).astype(jnp.float32) * (2.0 * math.pi / whole)
    side = (moved >> (quarter.bit_length() - 1)) & 3
    y = x * x
    s = x * (1.0 + y * (-1.0 / 6 + y * (1.0 / 120 + y * (-1.0 / 5040 + y * (1.0 / 362880)))))
    c = 1.0 + y * (-0.5 + y * (1.0 / 24 + y * (-1.0 / 720 + y * (1.0 / 40320))))
    odd = (side & 1) == 1
    cos = jnp.where(odd, s, c)
    sin = jnp.where(odd, c, s)
    cos = jnp.where((side == 1) | (side == 2), -cos, cos)
    sin = jnp.where(side >= 2, -sin, sin)
    return cos, sin


def beam_kernel(first_ref, delays_ref, r_ref, out_ref, step_cos, step_sin, mid_cos, mid_sin, left, power):
    sources, count, share, lanes = r_ref.shape
    stations, beams = delays_ref.shape
    half = lanes // 2
    width = 2 * LANES
    pairs = GROUP // 2

    @pl.when(pl.program_id(0) == 0)
    def _():
        def rows(t, carry):
            at = pl.ds(pl.multiple_of(t * ROWS, ROWS), ROWS)
            ch, sh = turn_of(delays_ref[at, :])
            c1, s1 = ch * ch - sh * sh, 2.0 * sh * ch
            for j in range(pairs):
                step_cos[j, at, :] = ch
                step_sin[j, at, :] = sh
                ch, sh = ch * c1 - sh * s1, sh * c1 + ch * s1
            return carry

        lax.fori_loop(0, stations // ROWS, rows, 0)

    twice = 2 * (first_ref[0] + GROUP * pl.program_id(0)) + GROUP - 1
    scale = 1.0 / math.sqrt(stations)

    def middle(t, carry):
        at = pl.ds(pl.multiple_of(t * ROWS, ROWS), ROWS)
        c, s = turn_of(delays_ref[at, :] * twice)
        mid_cos[at, :] = c * scale
        mid_sin[at, :] = s * scale
        return carry

    lax.fori_loop(0, stations // ROWS, middle, 0)

    def lay(k, carry):
        both = jnp.concatenate([r_ref[g, k].astype(jnp.float32) for g in range(sources)], 0).T
        left[k, 0] = both.astype(jnp.bfloat16)
        left[k, 1] = jnp.concatenate([both[half:], -both[:half]], 0).astype(jnp.bfloat16)
        return carry

    lax.fori_loop(0, count, lay, 0)

    def one(k, cos, sin):
        out = jnp.dot(left[k, 0], cos.astype(jnp.bfloat16), preferred_element_type=jnp.float32)
        out = out + jnp.dot(left[k, 1], sin.astype(jnp.bfloat16), preferred_element_type=jnp.float32)
        energy = (out * out).reshape(2 * INTEG, lanes // (2 * INTEG), width)
        return jnp.sum(energy, 0) * (1.0 / INTEG)

    def tile(step, carry):
        j, b = step // (beams // width), step % (beams // width)
        at = pl.ds(pl.multiple_of(b * width, width), width)
        cm, sm = mid_cos[:, at], mid_sin[:, at]
        cj, sj = step_cos[j, :, at], step_sin[j, :, at]
        cc, ss, sc, cs = cm * cj, sm * sj, sm * cj, cm * sj
        power[pairs + j, :, at] = one(pairs + j, cc - ss, sc + cs)
        power[pairs - 1 - j, :, at] = one(pairs - 1 - j, cc + ss, sc - cs)
        return carry

    lax.fori_loop(0, pairs * (beams // width), tile, 0)
    mine = out_ref.shape[3]
    for g in range(out_ref.shape[0]):
        out_ref[g] = power[:, :, g * mine : (g + 1) * mine].astype(jnp.bfloat16)


def beams_of(first, delays, received, owners):
    sources, count, share, lanes = received.shape
    stations, beams = delays.shape
    powers = lanes // (2 * INTEG)
    mine = beams // owners
    return pl.pallas_call(
        beam_kernel,
        grid=(count // GROUP,),
        in_specs=[
            pl.BlockSpec(memory_space=pltpu.SMEM),
            pl.BlockSpec(delays.shape, lambda i: (0, 0)),
            pl.BlockSpec((sources, GROUP, share, lanes), lambda i: (0, i, 0, 0)),
        ],
        out_specs=pl.BlockSpec((owners, GROUP, powers, mine), lambda i: (0, i, 0, 0)),
        out_shape=jax.ShapeDtypeStruct((owners, count, powers, mine), jnp.bfloat16),
        scratch_shapes=[
            pltpu.VMEM((GROUP // 2, stations, beams), jnp.float32),
            pltpu.VMEM((GROUP // 2, stations, beams), jnp.float32),
            pltpu.VMEM((stations, beams), jnp.float32),
            pltpu.VMEM((stations, beams), jnp.float32),
            pltpu.VMEM((GROUP, 2, lanes, stations), jnp.bfloat16),
            pltpu.VMEM((GROUP, powers, beams), jnp.float32),
        ],
        compiler_params=pltpu.CompilerParams(vmem_limit_bytes=VMEM_LIMIT),
        name="beams",
    )(first, delays, received)


def tree_kernel(shifts_ref, own_ref, next_ref, out_ref, ping, pong):
    slots, length, beams = own_ref.shape
    base = pl.program_id(0) * slots
    span = 2 * length
    ping[:, pl.ds(0, length), :] = own_ref[...].astype(jnp.float32)
    ping[:, pl.ds(length, length), :] = next_ref[...].astype(jnp.float32)
    zeros = jnp.zeros((slots, ROWS, beams), jnp.float32)
    ping[:, pl.ds(span, ROWS), :] = zeros
    pong[:, pl.ds(span, ROWS), :] = zeros
    src, dst = ping, pong
    for level in range(LEVELS):
        h = 2**level
        rows = span if level < LEVELS - 1 else length

        def tree(t, carry, src=src, dst=dst, h=h, rows=rows, level=level):
            start = t * GROUP
            for i in range(GROUP // 2):
                lead = start + i // h * 2 * h + i % h
                first = src[lead, pl.ds(0, rows), :]
                shifted = [src[lead + h, pl.ds(by, rows), :] for by in range(SHIFT_MOST + 1)]
                for c in (2 * i, 2 * i + 1):
                    amount = shifts_ref[level, base + start + c]
                    moved = shifted[SHIFT_MOST]
                    for by in range(SHIFT_MOST):
                        moved = jnp.where(amount == by, shifted[by], moved)
                    dst[start + c, pl.ds(0, rows), :] = first + moved
            return carry

        lax.fori_loop(0, slots // GROUP, tree, 0)
        src, dst = dst, src
    for t in range(length):
        out_ref[:, t, :] = (src[:, t, :] * 0.5**LEVELS).T


def dedisperse(shifts, own, after):
    slots, length, beams = own.shape
    block = LANES
    return pl.pallas_call(
        tree_kernel,
        grid=(slots // block,),
        in_specs=[
            pl.BlockSpec(memory_space=pltpu.SMEM),
            pl.BlockSpec((block, length, beams), lambda i: (i, 0, 0)),
            pl.BlockSpec((block, length, beams), lambda i: (i, 0, 0)),
        ],
        out_specs=pl.BlockSpec((beams, length, block), lambda i: (0, 0, i)),
        out_shape=jax.ShapeDtypeStruct((beams, length, slots), jnp.float32),
        scratch_shapes=[
            pltpu.VMEM((block, 2 * length + ROWS, beams), jnp.float32),
            pltpu.VMEM((block, 2 * length + ROWS, beams), jnp.float32),
        ],
        compiler_params=pltpu.CompilerParams(vmem_limit_bytes=VMEM_LIMIT),
        name="dedisperse",
    )(shifts, own, after)


def local(voltages, filter_taps, delays, shifts):
    owners = lax.axis_size("grp")
    halo = shift_along(voltages[:, :, voltages.shape[2] - (TAPS - 1) * TRANSFORM :], "tm", 1)
    spectra = channelize(voltages, halo, filter_taps, owners)
    share = spectra.shape[3]
    mine = CHANNELS // owners
    spectra = spectra.reshape(owners, mine * share, LANES)
    received = lax.all_to_all(spectra, "grp", split_axis=0, concat_axis=0, tiled=True)
    received = received.reshape(owners, mine, share, LANES)
    if share % ROWS:
        received = jnp.transpose(received, (1, 0, 2, 3)).reshape(1, mine, owners * share, LANES)
    first = (lax.axis_index("grp") * mine).astype(jnp.int32).reshape(1)
    powers = beams_of(first, delays, received, owners)
    owned = lax.all_to_all(powers, "grp", split_axis=0, concat_axis=0, tiled=True)
    owned = owned.reshape(CHANNELS, powers.shape[2], powers.shape[3])
    after = shift_along(owned, "tm", -1)
    return jnp.transpose(dedisperse(shifts, owned, after), (0, 2, 1))


def solution(mesh):
    placed = (P(None, "grp", "tm"), P(), P(), P())
    return jax.shard_map(
        local, mesh=mesh, in_specs=placed, out_specs=P("grp", None, "tm"), check_vma=False
    )
```

```python
import functools
import math

import jax
import jax.numpy as jnp
import numpy as np
from jax import lax
from jax.experimental import pallas as pl
from jax.experimental.pallas import tpu as pltpu
from jax.sharding import PartitionSpec as P

TRANSFORM = 4096
CHANNELS = 512
TAPS = 4
INTEG = 8
LEVELS = 4
SHIFT_MOST = 2

RADIX = 4
SUB = TRANSFORM // RADIX
PER = CHANNELS // RADIX
LANES = 128
WIDE = 2 * LANES
ROWS = 8
STEPS = 2
GROUP = 2**LEVELS
VMEM_LIMIT = 60 * 1024 * 1024


def shift_along(x, axis, by):
    length = lax.axis_size(axis)
    pairs = [(i, i + by) for i in range(length) if 0 <= i + by < length]
    return lax.ppermute(x, axis, pairs)


def table_factors():
    k = (RADIX * np.arange(PER)[None, :] + np.arange(RADIX)[:, None])[:, None, :]
    fine = k * np.arange(ROWS)[None, :, None] % TRANSFORM
    coarse = k * (ROWS * np.arange(SUB // ROWS))[None, :, None] % TRANSFORM
    turn = 2.0 * np.pi / TRANSFORM
    scale = 1.0 / math.sqrt(TRANSFORM)
    fine = np.stack([np.cos(fine * turn), np.sin(fine * turn)], 1)
    coarse = np.stack([np.cos(coarse * turn), np.sin(coarse * turn)], 1) * scale
    return fine.astype(np.float32), coarse.astype(np.float32)


def channel_kernel(frames, x_ref, halo_ref, taps_ref, fine_ref, coarse_ref, *refs):
    *out_refs, table, folded, spectra, turned, weights, rim = refs
    stations = x_ref.shape[1]
    here = x_ref.shape[2] // TRANSFORM
    step, steps = pl.program_id(1), pl.num_programs(1)

    @pl.when((pl.program_id(0) == 0) & (step == 0))
    def _():
        for p in range(TAPS):
            weights[p] = jnp.broadcast_to(taps_ref[p : p + 1, :], (ROWS, TRANSFORM)).astype(jnp.bfloat16)

        def build(u, carry):
            for q in range(RADIX):
                ca, sa = fine_ref[q, 0], fine_ref[q, 1]
                cs, ss = [], []
                for half in range(2):
                    cb = coarse_ref[q, 0, pl.ds(2 * u + half, 1), :]
                    sb = coarse_ref[q, 1, pl.ds(2 * u + half, 1), :]
                    cs.append(cb * ca - sb * sa)
                    ss.append(sb * ca + cb * sa)
                c = jnp.concatenate(cs, 0).astype(jnp.bfloat16)
                s = jnp.concatenate(ss, 0)
                top = pl.ds(pl.multiple_of(u * 2 * ROWS, 2 * ROWS), 2 * ROWS)
                low = pl.ds(pl.multiple_of(SUB + u * 2 * ROWS, 2 * ROWS), 2 * ROWS)
                table[q, top, :PER] = c
                table[q, top, PER:] = (-s).astype(jnp.bfloat16)
                table[q, low, :PER] = s.astype(jnp.bfloat16)
                table[q, low, PER:] = c
            return carry

        lax.fori_loop(0, SUB // (2 * ROWS), build, 0)

    @pl.when(step == 0)
    def _():
        rim[...] = halo_ref[...]

    def full(x):
        if stations < ROWS:
            x = jnp.concatenate([x, jnp.zeros((ROWS - stations, WIDE), x.dtype)], 0)
        return x

    parts = [(c, j) for c in range(2) for j in range(RADIX)]

    def columns(tile, carry):
        taps = [
            [weights[p, :, pl.ds(pl.multiple_of(j * SUB + tile * WIDE, WIDE), WIDE)] for j in range(RADIX)]
            for p in range(TAPS)
        ]

        def at(ref, f, c, j):
            start = pl.multiple_of(f * TRANSFORM + j * SUB + tile * WIDE, WIDE)
            return full(ref[c, :, pl.ds(start, WIDE)])

        def filtered(f, before):
            z, after = {}, []
            for (c, j), old in zip(parts, before):
                now = at(x_ref, f, c, j)
                total = taps[0][j] * now
                for p in range(1, TAPS):
                    total = total + taps[p][j] * old[p - 1]
                z[c, j] = total
                after.append((now, *old[:-1]))
            even = [z[c, 0] + z[c, 2] for c in range(2)]
            odd = [z[c, 0] - z[c, 2] for c in range(2)]
            even1 = [z[c, 1] + z[c, 3] for c in range(2)]
            odd1 = [z[c, 1] - z[c, 3] for c in range(2)]
            y = {
                (0, 0): even[0] + even1[0], (0, 1): even[1] + even1[1],
                (2, 0): even[0] - even1[0], (2, 1): even[1] - even1[1],
                (1, 0): odd[0] + odd1[1], (1, 1): odd[1] - odd1[0],
                (3, 0): odd[0] - odd1[1], (3, 1): odd[1] + odd1[0],
            }
            return y, after

        def pair(two, before):
            f = two * 2
            first, before = filtered(f, before)
            second, before = filtered(f + 1, before)
            rows = pl.ds(pl.multiple_of((step * here + f) * ROWS, 2 * ROWS), 2 * ROWS)
            for q in range(RADIX):
                for c in range(2):
                    both = jnp.concatenate([first[q, c], second[q, c]], 0)
                    lanes = pl.ds(pl.multiple_of(c * SUB + tile * WIDE, WIDE), WIDE)
                    folded[q, rows, lanes] = both.astype(jnp.bfloat16)
            return before

        before = [tuple(at(rim, TAPS - 2 - p, c, j) for p in range(TAPS - 1)) for c, j in parts]
        lax.fori_loop(0, here // 2, pair, before)
        return carry

    lax.fori_loop(0, SUB // WIDE, columns, 0)

    @pl.when(step < steps - 1)
    def _():
        rim[...] = x_ref[:, :, pl.ds((here - TAPS + 1) * TRANSFORM, (TAPS - 1) * TRANSFORM)]

    def transform(q):
        both = jnp.dot(folded[q], table[q], preferred_element_type=jnp.float32)
        spectra[q % 2, 0] = both[:, :PER]
        spectra[q % 2, 1] = both[:, PER:]

    def lay(q):
        powers = frames // INTEG
        for s in range(stations):
            rows = [
                spectra[q % 2, part, pl.ds(i * ROWS + s, powers, stride=INTEG * ROWS), :]
                for part in range(2)
                for i in range(INTEG)
            ]
            turned[q % 2, pl.ds(s, PER, stride=ROWS), :] = jnp.concatenate(rows, 0).T
        start = 0
        for out_ref in out_refs:
            owners, groups, per = out_ref.shape[:3]
            for n in range(groups):
                many = owners * per * ROWS
                block = turned[q % 2, start : start + many].reshape(owners, per, ROWS, LANES)
                out_ref[:, n, :, q] = block[:, :, :stations].astype(jnp.bfloat16)
                start += many

    @pl.when(step == steps - 1)
    def _():
        for q in range(RADIX + 1):
            if q < RADIX:
                transform(q)
            if q:
                lay(q - 1)


def channelize(voltages, halo, filter_taps, owners, first, last, pieces):
    stations = last - first
    frames = voltages.shape[2] // TRANSFORM
    block = ROWS if stations % ROWS == 0 else stations
    assert block <= ROWS and 2 * frames == LANES and first % block == 0
    offset = first // block
    per = GROUP // RADIX
    fine, coarse = table_factors()
    return pl.pallas_call(
        functools.partial(channel_kernel, frames),
        grid=(stations // block, STEPS),
        in_specs=[
            pl.BlockSpec((2, block, voltages.shape[2] // STEPS), lambda i, h: (0, i + offset, h)),
            pl.BlockSpec((2, block, halo.shape[2]), lambda i, h: (0, i, 0)),
            pl.BlockSpec(filter_taps.shape, lambda i, h: (0, 0)),
            pl.BlockSpec(fine.shape, lambda i, h: (0, 0, 0, 0)),
            pl.BlockSpec(coarse.shape, lambda i, h: (0, 0, 0, 0)),
        ],
        out_specs=[
            pl.BlockSpec((owners, n, per, RADIX, block, LANES), lambda i, h: (0, 0, 0, 0, i, 0)) for n in pieces
        ],
        out_shape=[
            jax.ShapeDtypeStruct((owners, n, per, RADIX, stations, LANES), jnp.bfloat16) for n in pieces
        ],
        scratch_shapes=[
            pltpu.VMEM((RADIX, 2 * SUB, 2 * PER), jnp.bfloat16),
            pltpu.VMEM((RADIX, frames * ROWS, 2 * SUB), jnp.bfloat16),
            pltpu.VMEM((2, 2, frames * ROWS, PER), jnp.float32),
            pltpu.VMEM((2, PER * ROWS, LANES), jnp.float32),
            pltpu.VMEM((TAPS, ROWS, TRANSFORM), jnp.bfloat16),
            pltpu.VMEM((2, block, (TAPS - 1) * TRANSFORM), jnp.bfloat16),
        ],
        compiler_params=pltpu.CompilerParams(vmem_limit_bytes=VMEM_LIMIT),
        cost_estimate=pl.CostEstimate(
            flops=stations * frames * 8 * SUB * CHANNELS, bytes_accessed=stations * 4 * voltages.shape[2], transcendentals=0
        ),
        name="channelize",
    )(voltages, halo, filter_taps, jnp.asarray(fine), jnp.asarray(coarse))


def turn_of(steps):
    whole = 2 * TRANSFORM
    quarter = whole // 4
    moved = (steps & (whole - 1)) + quarter // 2
    x = ((moved & (quarter - 1)) - quarter // 2).astype(jnp.float32) * (2.0 * math.pi / whole)
    side = (moved >> (quarter.bit_length() - 1)) & 3
    y = x * x
    s = x * (1.0 + y * (-1.0 / 6 + y * (1.0 / 120 + y * (-1.0 / 5040 + y * (1.0 / 362880)))))
    c = 1.0 + y * (-0.5 + y * (1.0 / 24 + y * (-1.0 / 720 + y * (1.0 / 40320))))
    odd = (side & 1) == 1
    cos = jnp.where(odd, s, c)
    sin = jnp.where(odd, c, s)
    cos = jnp.where((side == 1) | (side == 2), -cos, cos)
    sin = jnp.where(side >= 2, -sin, sin)
    return cos, sin


def packing(mine):
    whole, rest = divmod(mine, LANES)
    part = 1 << (rest - 1).bit_length() if rest else LANES
    share = part * GROUP // LANES if rest else 0
    return whole, rest, part, share


def turns(first, delays, owners, groups):
    stations, beams = delays.shape
    pairs = GROUP // 2

    def kernel(first_ref, delays_ref, step_ref, mid_ref):
        ch, sh = turn_of(delays_ref[...])
        twice = 2.0 * (ch * ch - sh * sh)
        before, now = (ch, -sh), (ch, sh)
        for j in range(pairs):
            step_ref[j, 0], step_ref[j, 1] = now
            before, now = now, (twice * now[0] - before[0], twice * now[1] - before[1])
        for a in range(groups):
            c, s = turn_of(delays_ref[...] * (2 * (first_ref[0] + owners * GROUP * a) + GROUP - 1))
            mid_ref[a, 0] = c * (1.0 / math.sqrt(stations))
            mid_ref[a, 1] = s * (1.0 / math.sqrt(stations))

    return pl.pallas_call(
        kernel,
        grid=(stations // ROWS,),
        in_specs=[
            pl.BlockSpec(memory_space=pltpu.SMEM),
            pl.BlockSpec((ROWS, beams), lambda i: (i, 0)),
        ],
        out_specs=[
            pl.BlockSpec((pairs, 2, ROWS, beams), lambda i: (0, 0, i, 0)),
            pl.BlockSpec((groups, 2, ROWS, beams), lambda i: (0, 0, i, 0)),
        ],
        out_shape=[
            jax.ShapeDtypeStruct((pairs, 2, stations, beams), jnp.float32),
            jax.ShapeDtypeStruct((groups, 2, stations, beams), jnp.float32),
        ],
        compiler_params=pltpu.CompilerParams(vmem_limit_bytes=VMEM_LIMIT),
        cost_estimate=pl.CostEstimate(
            flops=200 * stations * beams, bytes_accessed=8 * (pairs + groups) * stations * beams, transcendentals=0
        ),
        name="turns",
    )(first, delays)


def beam_kernel(step_ref, mid_ref, *refs):
    left, power = refs[-2:]
    *r_refs, out_ref = refs[:-2]
    lanes = r_refs[0].shape[3]
    _, _, beams = step_ref.shape
    half = lanes // 2
    width = 2 * LANES
    pairs = GROUP // 2
    j = pl.program_id(1)

    def lay(k, carry):
        both = [r[g, k].astype(jnp.float32) for r in r_refs for g in range(r.shape[0])]
        both = jnp.concatenate(both, 0).T
        left[k, 0] = both.astype(jnp.bfloat16)
        left[k, 1] = jnp.concatenate([both[half:], -both[:half]], 0).astype(jnp.bfloat16)
        return carry

    @pl.when(j == 0)
    def _():
        lax.fori_loop(0, GROUP, lay, 0)

    def one(k, cos, sin):
        out = jnp.dot(left[k, 0], cos.astype(jnp.bfloat16), preferred_element_type=jnp.float32)
        out = out + jnp.dot(left[k, 1], sin.astype(jnp.bfloat16), preferred_element_type=jnp.float32)
        energy = (out * out).reshape(2 * INTEG, lanes // (2 * INTEG), width)
        return jnp.sum(energy, 0) * (1.0 / INTEG)

    for b in range(beams // width):
        at = slice(b * width, (b + 1) * width)
        cm, sm = mid_ref[0, :, at], mid_ref[1, :, at]
        cj, sj = step_ref[0, :, at], step_ref[1, :, at]
        cc, ss, sc, cs = cm * cj, sm * sj, sm * cj, cm * sj
        power[pairs + j, :, at] = one(pairs + j, cc - ss, sc + cs)
        power[pairs - 1 - j, :, at] = one(pairs - 1 - j, cc + ss, sc - cs)
    mine = beams // out_ref.shape[0]
    whole, rest, part, share = packing(mine)

    @pl.when(j == pairs - 1)
    def _():
        for g in range(out_ref.shape[0]):
            own = power[:, :, g * mine : (g + 1) * mine]
            for t in range(whole):
                out_ref[g, t * GROUP : (t + 1) * GROUP] = own[:, :, t * LANES : (t + 1) * LANES].astype(jnp.bfloat16)
            if rest:
                tail = own[:, :, whole * LANES :]
                if part > rest:
                    tail = jnp.concatenate([tail, jnp.zeros((*tail.shape[:2], part - rest), tail.dtype)], 2)
                tail = jnp.concatenate([tail[m * share : (m + 1) * share] for m in range(LANES // part)], 2)
                out_ref[g, whole * GROUP :] = tail.astype(jnp.bfloat16)


def beams_of(steps, mids, received, owners, start, count):
    pairs, _, stations, beams = steps.shape
    lanes = received[0][0].shape[3]
    powers = lanes // (2 * INTEG)
    whole, _, _, share = packing(beams // owners)
    rows = whole * GROUP + share
    return pl.pallas_call(
        beam_kernel,
        grid=(count, pairs),
        in_specs=[
            pl.BlockSpec((None, 2, stations, beams), lambda i, j: (j, 0, 0, 0)),
            pl.BlockSpec((None, 2, stations, beams), lambda i, j: (i + start, 0, 0, 0)),
            *[
                pl.BlockSpec((r.shape[0], GROUP, r.shape[2], lanes), lambda i, j, at=at: (0, i + start - at, 0, 0))
                for r, at in received
            ],
        ],
        out_specs=pl.BlockSpec((owners, None, rows, powers, LANES), lambda i, j: (0, i, 0, 0, 0)),
        out_shape=jax.ShapeDtypeStruct((owners, count, rows, powers, LANES), jnp.bfloat16),
        scratch_shapes=[
            pltpu.VMEM((GROUP, 2, lanes, stations), jnp.bfloat16),
            pltpu.VMEM((GROUP, powers, beams), jnp.float32),
        ],
        compiler_params=pltpu.CompilerParams(vmem_limit_bytes=VMEM_LIMIT),
        cost_estimate=pl.CostEstimate(
            flops=8 * count * GROUP * beams * stations * lanes, bytes_accessed=4 * stations * beams, transcendentals=0
        ),
        name="beams",
    )(steps, mids, *[r for r, _ in received])


def tree_kernel(first_slot, beams, shifts_ref, own_ref, next_ref, *refs):
    out_ref, ping, pong = refs[-3:]
    sources, _, _, length, _ = own_ref.shape
    own_ref, next_ref = own_ref.at[:, 0], next_ref.at[:, 0]
    tiles, slots, depth, _ = ping.shape
    base = first_slot + (pl.program_id(0) * pl.num_programs(1) + pl.program_id(1)) * slots
    span = 2 * length
    whole, rest, part, share = packing(beams)
    zeros = jnp.zeros((tiles, slots, depth - span, LANES), jnp.float32)
    ping[:, :, pl.ds(span, depth - span), :] = zeros
    pong[:, :, pl.ds(span, depth - span), :] = zeros
    for ref, at in ((own_ref, 0), (next_ref, length)):
        for s in range(sources):
            for t in range(whole):
                block = ref[s, t * GROUP : (t + 1) * GROUP].astype(jnp.float32)
                ping[t, s * GROUP : (s + 1) * GROUP, pl.ds(at, length), :] = block
            if rest:
                block = ref[s, whole * GROUP :].astype(jnp.float32)
                for m in range(LANES // part):
                    low = s * GROUP + m * share
                    moved = pltpu.roll(block, LANES - m * part, 2) if m else block
                    ping[whole, low : low + share, pl.ds(at, length), :] = moved
    src, dst = ping, pong
    for level in range(LEVELS):
        h = 2**level
        rows = span if level < LEVELS - 1 else length

        def tree(t, carry, src=src, dst=dst, h=h, rows=rows, level=level):
            start = t * GROUP
            for i in range(GROUP // 2):
                lead = start + i // h * 2 * h + i % h
                amounts = [shifts_ref[level, base + start + 2 * i + r] for r in range(2)]
                for tile in range(tiles):
                    first = src[tile, lead, pl.ds(0, rows), :]
                    shifted = [src[tile, lead + h, pl.ds(by, rows), :] for by in range(SHIFT_MOST + 1)]
                    for r in range(2):
                        moved = shifted[SHIFT_MOST]
                        for by in range(SHIFT_MOST):
                            moved = jnp.where(amounts[r] == by, shifted[by], moved)
                        dst[tile, start + 2 * i + r, pl.ds(0, rows), :] = first + moved
            return carry

        lax.fori_loop(0, slots // GROUP, tree, 0)
        src, dst = dst, src
    for tile in range(tiles):
        flat = src.at[tile].reshape(slots * depth, LANES)
        here = min(LANES, beams - tile * LANES)
        for t in range(length):
            turned = (flat[pl.ds(t, slots, stride=depth), :] * 0.5**LEVELS).T
            out_ref[pl.ds(tile * LANES * length + t, here, stride=length), :] = turned[:here]


def dedisperse(shifts, own, after, beams, first_slot, total, so_far):
    sources, groups, rows, length, _ = own.shape
    block = LANES // GROUP
    blocks = sources // block
    tiles = pl.cdiv(beams, LANES)
    depth = 2 * length + ROWS
    earlier = [] if so_far is None else [so_far]
    return pl.pallas_call(
        functools.partial(tree_kernel, first_slot, beams),
        grid=(groups, blocks),
        in_specs=[
            pl.BlockSpec(memory_space=pltpu.SMEM),
            pl.BlockSpec((block, 1, rows, length, LANES), lambda a, i: (i, a, 0, 0, 0)),
            pl.BlockSpec((block, 1, rows, length, LANES), lambda a, i: (i, a, 0, 0, 0)),
            *[pl.BlockSpec(memory_space=pl.ANY) for _ in earlier],
        ],
        out_specs=pl.BlockSpec((beams * length, LANES), lambda a, i: (0, first_slot // LANES + a * blocks + i)),
        out_shape=jax.ShapeDtypeStruct((beams * length, total), jnp.float32),
        scratch_shapes=[pltpu.VMEM((tiles, LANES, depth, LANES), jnp.float32)] * 2,
        input_output_aliases={3: 0} if earlier else {},
        compiler_params=pltpu.CompilerParams(vmem_limit_bytes=VMEM_LIMIT),
        cost_estimate=pl.CostEstimate(
            flops=16 * beams * length * GROUP * sources * groups, bytes_accessed=10 * beams * length * GROUP * sources * groups, transcendentals=0
        ),
        name="dedisperse",
    )(shifts, own, after, *earlier)


def swapped(x, owners):
    return lax.all_to_all(x.reshape(owners, -1, LANES), "grp", split_axis=0, concat_axis=0, tiled=True)


def local(voltages, filter_taps, delays, shifts):
    owners = lax.axis_size("grp")
    share = voltages.shape[1]
    groups = CHANNELS // (owners * GROUP)
    length = voltages.shape[2] // TRANSFORM // INTEG
    beams = delays.shape[1] // owners
    rim = voltages.shape[2] - (TAPS - 1) * TRANSFORM
    cuts = [0, ROWS, share] if share > ROWS else [0, share]
    early = [groups // 2, groups - groups // 2] if groups > 1 else [groups]
    calls = [groups // 2] + [1] * (groups - groups // 2) if groups > 1 else [groups]
    halos = []
    for first, last in zip(cuts, cuts[1:]):
        halos.append(shift_along(voltages[:, first:last, rim:], "tm", 1))
    received = []
    for n, (first, last) in enumerate(zip(cuts, cuts[1:])):
        pieces = early if last == share else [groups]
        arrays = channelize(voltages, halos[n], filter_taps, owners, first, last, pieces)
        start = 0
        for many, array in zip(pieces, arrays):
            here = swapped(array, owners)
            here = here.reshape(owners, many * GROUP, last - first, LANES)
            if (last - first) % ROWS:
                here = jnp.transpose(here, (1, 0, 2, 3)).reshape(1, many * GROUP, -1, LANES)
            received.append((here, start, start + many))
            start += many
    by_owner = delays.reshape(owners, share, delays.shape[1])
    delays = jnp.concatenate([by_owner[:, a:b].reshape(-1, delays.shape[1]) for a, b in zip(cuts, cuts[1:])])
    mine = (lax.axis_index("grp") * GROUP).astype(jnp.int32).reshape(1)
    steps, mids = turns(mine, delays, owners, groups)
    out, start = None, 0
    for many in calls:
        arrays = [(r, low) for r, low, high in received if low <= start and start + many <= high]
        power = beams_of(steps, mids, arrays, owners, start, many)
        owned = swapped(power, owners).reshape(power.shape)
        after = shift_along(owned, "tm", -1)
        out = dedisperse(shifts, owned, after, beams, start * owners * GROUP, CHANNELS, out)
        start += many
    return jnp.transpose(out.reshape(beams, length, CHANNELS), (0, 2, 1))


def solution(mesh):
    placed = (P(None, "grp", "tm"), P(), P(), P())
    return jax.shard_map(local, mesh=mesh, in_specs=placed, out_specs=P("grp", None, "tm"), check_vma=False)
```

```python
import functools
import math

import jax
import jax.numpy as jnp
import numpy as np
from jax import lax
from jax.experimental import pallas as pl
from jax.experimental.pallas import tpu as pltpu
from jax.sharding import PartitionSpec as P

TRANSFORM = 4096
CHANNELS = 512
TAPS = 4
INTEG = 8
LEVELS = 4
SHIFT_MOST = 2

RADIX = 4
SUB = TRANSFORM // RADIX
PER = CHANNELS // RADIX
LANES = 128
WIDE = 2 * LANES
ROWS = 8
STEPS = 2
GROUP = 2**LEVELS
VMEM_LIMIT = 60 * 1024 * 1024


def shift_along(x, axis, by):
    length = lax.axis_size(axis)
    pairs = [(i, i + by) for i in range(length) if 0 <= i + by < length]
    return lax.ppermute(x, axis, pairs)


def table_factors():
    k = (RADIX * np.arange(PER)[None, :] + np.arange(RADIX)[:, None])[:, None, :]
    fine = k * np.arange(ROWS)[None, :, None] % TRANSFORM
    coarse = k * (ROWS * np.arange(SUB // ROWS))[None, :, None] % TRANSFORM
    turn = 2.0 * np.pi / TRANSFORM
    scale = 1.0 / math.sqrt(TRANSFORM)
    fine = np.stack([np.cos(fine * turn), np.sin(fine * turn)], 1)
    coarse = np.stack([np.cos(coarse * turn), np.sin(coarse * turn)], 1) * scale
    return fine.astype(np.float32), coarse.astype(np.float32)


def channel_kernel(frames, x_ref, halo_ref, taps_ref, fine_ref, coarse_ref, *refs):
    *out_refs, table, folded, spectra, turned, weights, rim = refs
    stations = x_ref.shape[1]
    here = x_ref.shape[2] // TRANSFORM
    step, steps = pl.program_id(1), pl.num_programs(1)

    @pl.when((pl.program_id(0) == 0) & (step == 0))
    def _():
        for p in range(TAPS):
            weights[p] = jnp.broadcast_to(taps_ref[p : p + 1, :], (ROWS, TRANSFORM)).astype(jnp.bfloat16)

        def build(u, carry):
            for q in range(RADIX):
                ca, sa = fine_ref[q, 0], fine_ref[q, 1]
                cs, ss = [], []
                for half in range(2):
                    cb = coarse_ref[q, 0, pl.ds(2 * u + half, 1), :]
                    sb = coarse_ref[q, 1, pl.ds(2 * u + half, 1), :]
                    cs.append(cb * ca - sb * sa)
                    ss.append(sb * ca + cb * sa)
                c = jnp.concatenate(cs, 0).astype(jnp.bfloat16)
                s = jnp.concatenate(ss, 0)
                top = pl.ds(pl.multiple_of(u * 2 * ROWS, 2 * ROWS), 2 * ROWS)
                low = pl.ds(pl.multiple_of(SUB + u * 2 * ROWS, 2 * ROWS), 2 * ROWS)
                table[q, top, :PER] = c
                table[q, top, PER:] = (-s).astype(jnp.bfloat16)
                table[q, low, :PER] = s.astype(jnp.bfloat16)
                table[q, low, PER:] = c
            return carry

        lax.fori_loop(0, SUB // (2 * ROWS), build, 0)

    @pl.when(step == 0)
    def _():
        rim[...] = halo_ref[...]

    def full(x):
        if stations < ROWS:
            x = jnp.concatenate([x, jnp.zeros((ROWS - stations, WIDE), x.dtype)], 0)
        return x

    parts = [(c, j) for c in range(2) for j in range(RADIX)]

    def columns(tile, carry):
        taps = [
            [weights[p, :, pl.ds(pl.multiple_of(j * SUB + tile * WIDE, WIDE), WIDE)] for j in range(RADIX)]
            for p in range(TAPS)
        ]

        def at(ref, f, c, j):
            start = pl.multiple_of(f * TRANSFORM + j * SUB + tile * WIDE, WIDE)
            return full(ref[c, :, pl.ds(start, WIDE)])

        def filtered(f, before):
            z, after = {}, []
            for (c, j), old in zip(parts, before):
                now = at(x_ref, f, c, j)
                total = taps[0][j] * now
                for p in range(1, TAPS):
                    total = total + taps[p][j] * old[p - 1]
                z[c, j] = total
                after.append((now, *old[:-1]))
            even = [z[c, 0] + z[c, 2] for c in range(2)]
            odd = [z[c, 0] - z[c, 2] for c in range(2)]
            even1 = [z[c, 1] + z[c, 3] for c in range(2)]
            odd1 = [z[c, 1] - z[c, 3] for c in range(2)]
            y = {
                (0, 0): even[0] + even1[0], (0, 1): even[1] + even1[1],
                (2, 0): even[0] - even1[0], (2, 1): even[1] - even1[1],
                (1, 0): odd[0] + odd1[1], (1, 1): odd[1] - odd1[0],
                (3, 0): odd[0] - odd1[1], (3, 1): odd[1] + odd1[0],
            }
            return y, after

        def pair(two, before):
            f = two * 2
            first, before = filtered(f, before)
            second, before = filtered(f + 1, before)
            rows = pl.ds(pl.multiple_of((step * here + f) * ROWS, 2 * ROWS), 2 * ROWS)
            for q in range(RADIX):
                for c in range(2):
                    both = jnp.concatenate([first[q, c], second[q, c]], 0)
                    lanes = pl.ds(pl.multiple_of(c * SUB + tile * WIDE, WIDE), WIDE)
                    folded[q, rows, lanes] = both.astype(jnp.bfloat16)
            return before

        before = [tuple(at(rim, TAPS - 2 - p, c, j) for p in range(TAPS - 1)) for c, j in parts]
        lax.fori_loop(0, here // 2, pair, before)
        return carry

    lax.fori_loop(0, SUB // WIDE, columns, 0)

    @pl.when(step < steps - 1)
    def _():
        rim[...] = x_ref[:, :, pl.ds((here - TAPS + 1) * TRANSFORM, (TAPS - 1) * TRANSFORM)]

    def transform(q):
        both = jnp.dot(folded[q], table[q], preferred_element_type=jnp.float32)
        spectra[q % 2, 0] = both[:, :PER]
        spectra[q % 2, 1] = both[:, PER:]

    def lay(q):
        powers = frames // INTEG
        for s in range(stations):
            rows = [
                spectra[q % 2, part, pl.ds(i * ROWS + s, powers, stride=INTEG * ROWS), :]
                for part in range(2)
                for i in range(INTEG)
            ]
            turned[q % 2, pl.ds(s, PER, stride=ROWS), :] = jnp.concatenate(rows, 0).T
        start = 0
        for out_ref in out_refs:
            owners, groups, per = out_ref.shape[:3]
            for n in range(groups):
                many = owners * per * ROWS
                block = turned[q % 2, start : start + many].reshape(owners, per, ROWS, LANES)
                out_ref[:, n, :, q] = block[:, :, :stations].astype(jnp.bfloat16)
                start += many

    @pl.when(step == steps - 1)
    def _():
        for q in range(RADIX + 1):
            if q < RADIX:
                transform(q)
            if q:
                lay(q - 1)


def channelize(voltages, halo, filter_taps, owners, first, last, pieces):
    stations = last - first
    frames = voltages.shape[2] // TRANSFORM
    block = ROWS if stations % ROWS == 0 else stations
    assert block <= ROWS and 2 * frames == LANES and first % block == 0
    offset = first // block
    per = GROUP // RADIX
    fine, coarse = table_factors()
    return pl.pallas_call(
        functools.partial(channel_kernel, frames),
        grid=(stations // block, STEPS),
        in_specs=[
            pl.BlockSpec((2, block, voltages.shape[2] // STEPS), lambda i, h: (0, i + offset, h)),
            pl.BlockSpec((2, block, halo.shape[2]), lambda i, h: (0, i, 0)),
            pl.BlockSpec(filter_taps.shape, lambda i, h: (0, 0)),
            pl.BlockSpec(fine.shape, lambda i, h: (0, 0, 0, 0)),
            pl.BlockSpec(coarse.shape, lambda i, h: (0, 0, 0, 0)),
        ],
        out_specs=[
            pl.BlockSpec((owners, n, per, RADIX, block, LANES), lambda i, h: (0, 0, 0, 0, i, 0)) for n in pieces
        ],
        out_shape=[
            jax.ShapeDtypeStruct((owners, n, per, RADIX, stations, LANES), jnp.bfloat16) for n in pieces
        ],
        scratch_shapes=[
            pltpu.VMEM((RADIX, 2 * SUB, 2 * PER), jnp.bfloat16),
            pltpu.VMEM((RADIX, frames * ROWS, 2 * SUB), jnp.bfloat16),
            pltpu.VMEM((2, 2, frames * ROWS, PER), jnp.float32),
            pltpu.VMEM((2, PER * ROWS, LANES), jnp.float32),
            pltpu.VMEM((TAPS, ROWS, TRANSFORM), jnp.bfloat16),
            pltpu.VMEM((2, block, (TAPS - 1) * TRANSFORM), jnp.bfloat16),
        ],
        compiler_params=pltpu.CompilerParams(vmem_limit_bytes=VMEM_LIMIT),
        cost_estimate=pl.CostEstimate(
            flops=stations * frames * 8 * SUB * CHANNELS, bytes_accessed=stations * 4 * voltages.shape[2], transcendentals=0
        ),
        name="channelize",
    )(voltages, halo, filter_taps, jnp.asarray(fine), jnp.asarray(coarse))


def turn_of(steps):
    whole = 2 * TRANSFORM
    quarter = whole // 4
    moved = (steps & (whole - 1)) + quarter // 2
    x = ((moved & (quarter - 1)) - quarter // 2).astype(jnp.float32) * (2.0 * math.pi / whole)
    side = (moved >> (quarter.bit_length() - 1)) & 3
    y = x * x
    s = x * (1.0 + y * (-1.0 / 6 + y * (1.0 / 120 + y * (-1.0 / 5040 + y * (1.0 / 362880)))))
    c = 1.0 + y * (-0.5 + y * (1.0 / 24 + y * (-1.0 / 720 + y * (1.0 / 40320))))
    odd = (side & 1) == 1
    cos = jnp.where(odd, s, c)
    sin = jnp.where(odd, c, s)
    cos = jnp.where((side == 1) | (side == 2), -cos, cos)
    sin = jnp.where(side >= 2, -sin, sin)
    return cos, sin


def packing(mine):
    whole, rest = divmod(mine, LANES)
    part = 1 << (rest - 1).bit_length() if rest else LANES
    share = part * GROUP // LANES if rest else 0
    return whole, rest, part, share


def turns(first, delays, owners, groups):
    stations, beams = delays.shape
    pairs = GROUP // 2

    def kernel(first_ref, delays_ref, step_ref, mid_ref):
        ch, sh = turn_of(delays_ref[...])
        twice = 2.0 * (ch * ch - sh * sh)
        before, now = (ch, -sh), (ch, sh)
        for j in range(pairs):
            step_ref[j, 0] = now[0].astype(jnp.bfloat16)
            step_ref[j, 1] = now[1].astype(jnp.bfloat16)
            before, now = now, (twice * now[0] - before[0], twice * now[1] - before[1])
        for a in range(groups):
            c, s = turn_of(delays_ref[...] * (2 * (first_ref[0] + owners * GROUP * a) + GROUP - 1))
            mid_ref[a, 0] = (c * (1.0 / math.sqrt(stations))).astype(jnp.bfloat16)
            mid_ref[a, 1] = (s * (1.0 / math.sqrt(stations))).astype(jnp.bfloat16)

    return pl.pallas_call(
        kernel,
        grid=(stations // (2 * ROWS),),
        in_specs=[
            pl.BlockSpec(memory_space=pltpu.SMEM),
            pl.BlockSpec((2 * ROWS, beams), lambda i: (i, 0)),
        ],
        out_specs=[
            pl.BlockSpec((pairs, 2, 2 * ROWS, beams), lambda i: (0, 0, i, 0)),
            pl.BlockSpec((groups, 2, 2 * ROWS, beams), lambda i: (0, 0, i, 0)),
        ],
        out_shape=[
            jax.ShapeDtypeStruct((pairs, 2, stations, beams), jnp.bfloat16),
            jax.ShapeDtypeStruct((groups, 2, stations, beams), jnp.bfloat16),
        ],
        compiler_params=pltpu.CompilerParams(vmem_limit_bytes=VMEM_LIMIT),
        cost_estimate=pl.CostEstimate(
            flops=200 * stations * beams, bytes_accessed=4 * (pairs + groups) * stations * beams, transcendentals=0
        ),
        name="turns",
    )(first, delays)


def beam_kernel(step_ref, mid_ref, *refs):
    left, power = refs[-2:]
    *r_refs, out_ref = refs[:-2]
    lanes = r_refs[0].shape[3]
    _, _, beams = step_ref.shape
    half = lanes // 2
    width = 2 * LANES
    pairs = GROUP // 2
    j = pl.program_id(1)

    def lay(k, carry):
        both = [r[g, k].astype(jnp.float32) for r in r_refs for g in range(r.shape[0])]
        both = jnp.concatenate(both, 0).T
        left[k, 0] = both.astype(jnp.bfloat16)
        left[k, 1] = jnp.concatenate([both[half:], -both[:half]], 0).astype(jnp.bfloat16)
        return carry

    @pl.when(j == 0)
    def _():
        lax.fori_loop(0, GROUP, lay, 0, unroll=4)

    def one(k, cos, sin):
        out = jnp.dot(left[k, 0], cos.astype(jnp.bfloat16), preferred_element_type=jnp.float32)
        out = out + jnp.dot(left[k, 1], sin.astype(jnp.bfloat16), preferred_element_type=jnp.float32)
        energy = (out * out).reshape(2 * INTEG, lanes // (2 * INTEG), width)
        return jnp.sum(energy, 0) * (1.0 / INTEG)

    for b in range(beams // width):
        at = slice(b * width, (b + 1) * width)
        cm, sm = mid_ref[0, :, at], mid_ref[1, :, at]
        cj, sj = step_ref[0, :, at], step_ref[1, :, at]
        cc, ss, sc, cs = cm * cj, sm * sj, sm * cj, cm * sj
        power[pairs + j, :, at] = one(pairs + j, cc - ss, sc + cs)
        power[pairs - 1 - j, :, at] = one(pairs - 1 - j, cc + ss, sc - cs)
    mine = beams // out_ref.shape[0]
    whole, rest, part, share = packing(mine)

    @pl.when(j == pairs - 1)
    def _():
        for g in range(out_ref.shape[0]):
            own = power[:, :, g * mine : (g + 1) * mine]
            for t in range(whole):
                out_ref[g, t * GROUP : (t + 1) * GROUP] = own[:, :, t * LANES : (t + 1) * LANES].astype(jnp.bfloat16)
            if rest:
                tail = own[:, :, whole * LANES :]
                if part > rest:
                    tail = jnp.concatenate([tail, jnp.zeros((*tail.shape[:2], part - rest), tail.dtype)], 2)
                tail = jnp.concatenate([tail[m * share : (m + 1) * share] for m in range(LANES // part)], 2)
                out_ref[g, whole * GROUP :] = tail.astype(jnp.bfloat16)


def beams_of(steps, mids, received, owners, start, count):
    pairs, _, stations, beams = steps.shape
    lanes = received[0][0].shape[3]
    powers = lanes // (2 * INTEG)
    whole, _, _, share = packing(beams // owners)
    rows = whole * GROUP + share
    return pl.pallas_call(
        beam_kernel,
        grid=(count, pairs),
        in_specs=[
            pl.BlockSpec((None, 2, stations, beams), lambda i, j: (j, 0, 0, 0)),
            pl.BlockSpec((None, 2, stations, beams), lambda i, j: (i + start, 0, 0, 0)),
            *[
                pl.BlockSpec((r.shape[0], GROUP, r.shape[2], lanes), lambda i, j, at=at: (0, i + start - at, 0, 0))
                for r, at in received
            ],
        ],
        out_specs=pl.BlockSpec((owners, None, rows, powers, LANES), lambda i, j: (0, i, 0, 0, 0)),
        out_shape=jax.ShapeDtypeStruct((owners, count, rows, powers, LANES), jnp.bfloat16),
        scratch_shapes=[
            pltpu.VMEM((GROUP, 2, lanes, stations), jnp.bfloat16),
            pltpu.VMEM((GROUP, powers, beams), jnp.float32),
        ],
        compiler_params=pltpu.CompilerParams(vmem_limit_bytes=VMEM_LIMIT),
        cost_estimate=pl.CostEstimate(
            flops=8 * count * GROUP * beams * stations * lanes, bytes_accessed=4 * stations * beams, transcendentals=0
        ),
        name="beams",
    )(steps, mids, *[r for r, _ in received])


def tree_kernel(first_slot, beams, shifts_ref, own_ref, next_ref, *refs):
    out_ref, ping, pong = refs[-3:]
    sources, _, _, length, _ = own_ref.shape
    own_ref, next_ref = own_ref.at[:, 0], next_ref.at[:, 0]
    tiles, slots, depth, _ = ping.shape
    base = first_slot + (pl.program_id(0) * pl.num_programs(1) + pl.program_id(1)) * slots
    span = 2 * length
    whole, rest, part, share = packing(beams)
    zeros = jnp.zeros((tiles, slots, depth - span, LANES), jnp.float32)
    ping[:, :, pl.ds(span, depth - span), :] = zeros
    pong[:, :, pl.ds(span, depth - span), :] = zeros
    for ref, at in ((own_ref, 0), (next_ref, length)):
        for s in range(sources):
            for t in range(whole):
                block = ref[s, t * GROUP : (t + 1) * GROUP].astype(jnp.float32)
                ping[t, s * GROUP : (s + 1) * GROUP, pl.ds(at, length), :] = block
            if rest:
                block = ref[s, whole * GROUP :].astype(jnp.float32)
                for m in range(LANES // part):
                    low = s * GROUP + m * share
                    moved = pltpu.roll(block, LANES - m * part, 2) if m else block
                    ping[whole, low : low + share, pl.ds(at, length), :] = moved
    src, dst = ping, pong
    for level in range(LEVELS):
        h = 2**level
        rows = span if level < LEVELS - 1 else length

        def tree(t, carry, src=src, dst=dst, h=h, rows=rows, level=level):
            start = t * GROUP
            for i in range(GROUP // 2):
                lead = start + i // h * 2 * h + i % h
                amounts = [shifts_ref[level, base + start + 2 * i + r] for r in range(2)]
                for tile in range(tiles):
                    first = src[tile, lead, pl.ds(0, rows), :]
                    shifted = [src[tile, lead + h, pl.ds(by, rows), :] for by in range(SHIFT_MOST + 1)]
                    for r in range(2):
                        moved = shifted[SHIFT_MOST]
                        for by in range(SHIFT_MOST):
                            moved = jnp.where(amounts[r] == by, shifted[by], moved)
                        dst[tile, start + 2 * i + r, pl.ds(0, rows), :] = first + moved
            return carry

        lax.fori_loop(0, slots // GROUP, tree, 0)
        src, dst = dst, src
    for tile in range(tiles):
        flat = src.at[tile].reshape(slots * depth, LANES)
        here = min(LANES, beams - tile * LANES)
        for t in range(length):
            turned = (flat[pl.ds(t, slots, stride=depth), :] * 0.5**LEVELS).T
            out_ref[pl.ds(tile * LANES * length + t, here, stride=length), :] = turned[:here]


def dedisperse(shifts, own, after, beams, first_slot, total, so_far):
    sources, groups, rows, length, _ = own.shape
    block = LANES // GROUP
    blocks = sources // block
    tiles = pl.cdiv(beams, LANES)
    depth = 2 * length + ROWS
    earlier = [] if so_far is None else [so_far]
    return pl.pallas_call(
        functools.partial(tree_kernel, first_slot, beams),
        grid=(groups, blocks),
        in_specs=[
            pl.BlockSpec(memory_space=pltpu.SMEM),
            pl.BlockSpec((block, 1, rows, length, LANES), lambda a, i: (i, a, 0, 0, 0)),
            pl.BlockSpec((block, 1, rows, length, LANES), lambda a, i: (i, a, 0, 0, 0)),
            *[pl.BlockSpec(memory_space=pl.ANY) for _ in earlier],
        ],
        out_specs=pl.BlockSpec((beams * length, LANES), lambda a, i: (0, first_slot // LANES + a * blocks + i)),
        out_shape=jax.ShapeDtypeStruct((beams * length, total), jnp.float32),
        scratch_shapes=[pltpu.VMEM((tiles, LANES, depth, LANES), jnp.float32)] * 2,
        input_output_aliases={3: 0} if earlier else {},
        compiler_params=pltpu.CompilerParams(vmem_limit_bytes=VMEM_LIMIT),
        cost_estimate=pl.CostEstimate(
            flops=16 * beams * length * GROUP * sources * groups, bytes_accessed=10 * beams * length * GROUP * sources * groups, transcendentals=0
        ),
        name="dedisperse",
    )(shifts, own, after, *earlier)


def swapped(x, owners):
    return lax.all_to_all(x.reshape(owners, -1, LANES), "grp", split_axis=0, concat_axis=0, tiled=True)


def local(voltages, filter_taps, delays, shifts):
    owners = lax.axis_size("grp")
    share = voltages.shape[1]
    groups = CHANNELS // (owners * GROUP)
    length = voltages.shape[2] // TRANSFORM // INTEG
    beams = delays.shape[1] // owners
    rim = voltages.shape[2] - (TAPS - 1) * TRANSFORM
    cuts = [0, ROWS, share] if share > ROWS else [0, share]
    early = [groups // 2, groups - groups // 2] if groups > 1 else [groups]
    calls = [groups // 2] + [1] * (groups - groups // 2) if groups > 1 else [groups]
    halos = []
    for first, last in zip(cuts, cuts[1:]):
        halos.append(shift_along(voltages[:, first:last, rim:], "tm", 1))
    received = []
    for n, (first, last) in enumerate(zip(cuts, cuts[1:])):
        pieces = early if last == share else [groups]
        arrays = channelize(voltages, halos[n], filter_taps, owners, first, last, pieces)
        start = 0
        for many, array in zip(pieces, arrays):
            here = swapped(array, owners)
            here = here.reshape(owners, many * GROUP, last - first, LANES)
            if (last - first) % ROWS:
                here = jnp.transpose(here, (1, 0, 2, 3)).reshape(1, many * GROUP, -1, LANES)
            received.append((here, start, start + many))
            start += many
    by_owner = delays.reshape(owners, share, delays.shape[1])
    delays = jnp.concatenate([by_owner[:, a:b].reshape(-1, delays.shape[1]) for a, b in zip(cuts, cuts[1:])])
    mine = (lax.axis_index("grp") * GROUP).astype(jnp.int32).reshape(1)
    steps, mids = turns(mine, delays, owners, groups)
    out, start = None, 0
    for many in calls:
        arrays = [(r, low) for r, low, high in received if low <= start and start + many <= high]
        power = beams_of(steps, mids, arrays, owners, start, many)
        owned = swapped(power, owners).reshape(power.shape)
        after = shift_along(owned, "tm", -1)
        out = dedisperse(shifts, owned, after, beams, start * owners * GROUP, CHANNELS, out)
        start += many
    return jnp.transpose(out.reshape(beams, length, CHANNELS), (0, 2, 1))


def solution(mesh):
    placed = (P(None, "grp", "tm"), P(), P(), P())
    return jax.shard_map(local, mesh=mesh, in_specs=placed, out_specs=P("grp", None, "tm"), check_vma=False)
```

```python
import functools
import math

import jax
import jax.numpy as jnp
import numpy as np
from jax import lax
from jax.experimental import pallas as pl
from jax.experimental.pallas import tpu as pltpu
from jax.sharding import PartitionSpec as P

TRANSFORM = 4096
CHANNELS = 512
TAPS = 4
INTEG = 8
LEVELS = 4
SHIFT_MOST = 2

RADIX = 4
SUB = TRANSFORM // RADIX
PER = CHANNELS // RADIX
LANES = 128
WIDE = 2 * LANES
ROWS = 8
STEPS = 2
GROUP = 2**LEVELS
MIB = 1024 * 1024


def shift_along(x, axis, by):
    length = lax.axis_size(axis)
    pairs = [(i, i + by) for i in range(length) if 0 <= i + by < length]
    return lax.ppermute(x, axis, pairs)


def table_factors():
    k = (RADIX * np.arange(PER)[None, :] + np.arange(RADIX)[:, None])[:, None, :]
    fine = k * np.arange(ROWS)[None, :, None] % TRANSFORM
    coarse = k * (ROWS * np.arange(SUB // ROWS))[None, :, None] % TRANSFORM
    turn = 2.0 * np.pi / TRANSFORM
    scale = 1.0 / math.sqrt(TRANSFORM)
    fine = np.stack([np.cos(fine * turn), np.sin(fine * turn)], 1)
    coarse = np.stack([np.cos(coarse * turn), np.sin(coarse * turn)], 1) * scale
    return fine.astype(np.float32), coarse.astype(np.float32)


def channel_kernel(frames, x_ref, halo_ref, taps_ref, fine_ref, coarse_ref, *refs):
    *out_refs, table, folded, spectra, turned, weights, rim = refs
    stations = x_ref.shape[1]
    here = x_ref.shape[2] // TRANSFORM
    step, steps = pl.program_id(1), pl.num_programs(1)

    @pl.when((pl.program_id(0) == 0) & (step == 0))
    def _():
        for p in range(TAPS):
            weights[p] = jnp.broadcast_to(taps_ref[p : p + 1, :], (ROWS, TRANSFORM)).astype(jnp.bfloat16)

        def build(u, carry):
            for q in range(RADIX):
                ca, sa = fine_ref[q, 0], fine_ref[q, 1]
                cs, ss = [], []
                for half in range(2):
                    cb = coarse_ref[q, 0, pl.ds(2 * u + half, 1), :]
                    sb = coarse_ref[q, 1, pl.ds(2 * u + half, 1), :]
                    cs.append(cb * ca - sb * sa)
                    ss.append(sb * ca + cb * sa)
                c = jnp.concatenate(cs, 0).astype(jnp.bfloat16)
                s = jnp.concatenate(ss, 0)
                top = pl.ds(pl.multiple_of(u * 2 * ROWS, 2 * ROWS), 2 * ROWS)
                low = pl.ds(pl.multiple_of(SUB + u * 2 * ROWS, 2 * ROWS), 2 * ROWS)
                table[q, top, :PER] = c
                table[q, top, PER:] = (-s).astype(jnp.bfloat16)
                table[q, low, :PER] = s.astype(jnp.bfloat16)
                table[q, low, PER:] = c
            return carry

        lax.fori_loop(0, SUB // (2 * ROWS), build, 0)

    @pl.when(step == 0)
    def _():
        rim[...] = halo_ref[...]

    def full(x):
        if stations < ROWS:
            x = jnp.concatenate([x, jnp.zeros((ROWS - stations, WIDE), x.dtype)], 0)
        return x

    parts = [(c, j) for c in range(2) for j in range(RADIX)]

    def columns(tile, carry):
        taps = [
            [weights[p, :, pl.ds(pl.multiple_of(j * SUB + tile * WIDE, WIDE), WIDE)] for j in range(RADIX)]
            for p in range(TAPS)
        ]

        def at(ref, f, c, j):
            start = pl.multiple_of(f * TRANSFORM + j * SUB + tile * WIDE, WIDE)
            return full(ref[c, :, pl.ds(start, WIDE)])

        def filtered(f, before):
            z, after = {}, []
            for (c, j), old in zip(parts, before):
                now = at(x_ref, f, c, j)
                total = taps[0][j] * now
                for p in range(1, TAPS):
                    total = total + taps[p][j] * old[p - 1]
                z[c, j] = total
                after.append((now, *old[:-1]))
            even = [z[c, 0] + z[c, 2] for c in range(2)]
            odd = [z[c, 0] - z[c, 2] for c in range(2)]
            even1 = [z[c, 1] + z[c, 3] for c in range(2)]
            odd1 = [z[c, 1] - z[c, 3] for c in range(2)]
            y = {
                (0, 0): even[0] + even1[0], (0, 1): even[1] + even1[1],
                (2, 0): even[0] - even1[0], (2, 1): even[1] - even1[1],
                (1, 0): odd[0] + odd1[1], (1, 1): odd[1] - odd1[0],
                (3, 0): odd[0] - odd1[1], (3, 1): odd[1] + odd1[0],
            }
            return y, after

        def pair(two, before):
            f = two * 2
            first, before = filtered(f, before)
            second, before = filtered(f + 1, before)
            rows = pl.ds(pl.multiple_of((step * here + f) * ROWS, 2 * ROWS), 2 * ROWS)
            for q in range(RADIX):
                for c in range(2):
                    both = jnp.concatenate([first[q, c], second[q, c]], 0)
                    lanes = pl.ds(pl.multiple_of(c * SUB + tile * WIDE, WIDE), WIDE)
                    folded[q, rows, lanes] = both.astype(jnp.bfloat16)
            return before

        before = [tuple(at(rim, TAPS - 2 - p, c, j) for p in range(TAPS - 1)) for c, j in parts]
        lax.fori_loop(0, here // 2, pair, before)
        return carry

    lax.fori_loop(0, SUB // WIDE, columns, 0)

    @pl.when(step < steps - 1)
    def _():
        rim[...] = x_ref[:, :, pl.ds((here - TAPS + 1) * TRANSFORM, (TAPS - 1) * TRANSFORM)]

    def transform(q):
        both = jnp.dot(folded[q], table[q], preferred_element_type=jnp.float32)
        spectra[q % 2, 0] = both[:, :PER]
        spectra[q % 2, 1] = both[:, PER:]

    def lay(q):
        powers = frames // INTEG
        for s in range(stations):
            rows = [
                spectra[q % 2, part, pl.ds(i * ROWS + s, powers, stride=INTEG * ROWS), :]
                for part in range(2)
                for i in range(INTEG)
            ]
            turned[q % 2, pl.ds(s, PER, stride=ROWS), :] = jnp.concatenate(rows, 0).T
        start = 0
        for out_ref in out_refs:
            owners, groups, per = out_ref.shape[:3]
            for n in range(groups):
                many = owners * per * ROWS
                block = turned[q % 2, start : start + many].reshape(owners, per, ROWS, LANES)
                out_ref[:, n, :, q] = block[:, :, :stations].astype(jnp.bfloat16)
                start += many

    @pl.when(step == steps - 1)
    def _():
        for q in range(RADIX + 1):
            if q < RADIX:
                transform(q)
            if q:
                lay(q - 1)


def channelize(voltages, halo, filter_taps, owners, first, last, pieces):
    stations = last - first
    frames = voltages.shape[2] // TRANSFORM
    block = ROWS if stations % ROWS == 0 else stations
    assert block <= ROWS and 2 * frames == LANES and first % block == 0
    offset = first // block
    per = GROUP // RADIX
    fine, coarse = table_factors()
    return pl.pallas_call(
        functools.partial(channel_kernel, frames),
        grid=(stations // block, STEPS),
        in_specs=[
            pl.BlockSpec((2, block, voltages.shape[2] // STEPS), lambda i, h: (0, i + offset, h)),
            pl.BlockSpec((2, block, halo.shape[2]), lambda i, h: (0, i, 0)),
            pl.BlockSpec(filter_taps.shape, lambda i, h: (0, 0)),
            pl.BlockSpec(fine.shape, lambda i, h: (0, 0, 0, 0)),
            pl.BlockSpec(coarse.shape, lambda i, h: (0, 0, 0, 0)),
        ],
        out_specs=[
            pl.BlockSpec((owners, n, per, RADIX, block, LANES), lambda i, h: (0, 0, 0, 0, i, 0)) for n in pieces
        ],
        out_shape=[
            jax.ShapeDtypeStruct((owners, n, per, RADIX, stations, LANES), jnp.bfloat16) for n in pieces
        ],
        scratch_shapes=[
            pltpu.VMEM((RADIX, 2 * SUB, 2 * PER), jnp.bfloat16),
            pltpu.VMEM((RADIX, frames * ROWS, 2 * SUB), jnp.bfloat16),
            pltpu.VMEM((2, 2, frames * ROWS, PER), jnp.float32),
            pltpu.VMEM((2, PER * ROWS, LANES), jnp.float32),
            pltpu.VMEM((TAPS, ROWS, TRANSFORM), jnp.bfloat16),
            pltpu.VMEM((2, block, (TAPS - 1) * TRANSFORM), jnp.bfloat16),
        ],
        compiler_params=pltpu.CompilerParams(vmem_limit_bytes=40 * MIB),
        cost_estimate=pl.CostEstimate(
            flops=stations * frames * 8 * SUB * CHANNELS, bytes_accessed=stations * 4 * voltages.shape[2], transcendentals=0
        ),
        name="channelize",
    )(voltages, halo, filter_taps, jnp.asarray(fine), jnp.asarray(coarse))


def turn_of(steps):
    whole = 2 * TRANSFORM
    quarter = whole // 4
    moved = (steps & (whole - 1)) + quarter // 2
    x = ((moved & (quarter - 1)) - quarter // 2).astype(jnp.float32) * (2.0 * math.pi / whole)
    side = (moved >> (quarter.bit_length() - 1)) & 3
    y = x * x
    s = x * (1.0 + y * (-1.0 / 6 + y * (1.0 / 120 + y * (-1.0 / 5040 + y * (1.0 / 362880)))))
    c = 1.0 + y * (-0.5 + y * (1.0 / 24 + y * (-1.0 / 720 + y * (1.0 / 40320))))
    odd = (side & 1) == 1
    cos = jnp.where(odd, s, c)
    sin = jnp.where(odd, c, s)
    cos = jnp.where((side == 1) | (side == 2), -cos, cos)
    sin = jnp.where(side >= 2, -sin, sin)
    return cos, sin


def packing(mine):
    whole, rest = divmod(mine, LANES)
    part = 1 << (rest - 1).bit_length() if rest else LANES
    share = part * GROUP // LANES if rest else 0
    return whole, rest, part, share


def turns(first, delays, owners, groups):
    stations, beams = delays.shape
    pairs = GROUP // 2

    def kernel(first_ref, delays_ref, step_ref, mid_ref):
        ch, sh = turn_of(delays_ref[...])
        twice = 2.0 * (ch * ch - sh * sh)
        before, now = (ch, -sh), (ch, sh)
        for j in range(pairs):
            step_ref[j, 0] = now[0].astype(jnp.bfloat16)
            step_ref[j, 1] = now[1].astype(jnp.bfloat16)
            before, now = now, (twice * now[0] - before[0], twice * now[1] - before[1])
        for a in range(groups):
            c, s = turn_of(delays_ref[...] * (2 * (first_ref[0] + owners * GROUP * a) + GROUP - 1))
            mid_ref[a, 0] = (c * (1.0 / math.sqrt(stations))).astype(jnp.bfloat16)
            mid_ref[a, 1] = (s * (1.0 / math.sqrt(stations))).astype(jnp.bfloat16)

    return pl.pallas_call(
        kernel,
        grid=(stations // (2 * ROWS),),
        in_specs=[
            pl.BlockSpec(memory_space=pltpu.SMEM),
            pl.BlockSpec((2 * ROWS, beams), lambda i: (i, 0)),
        ],
        out_specs=[
            pl.BlockSpec((pairs, 2, 2 * ROWS, beams), lambda i: (0, 0, i, 0)),
            pl.BlockSpec((groups, 2, 2 * ROWS, beams), lambda i: (0, 0, i, 0)),
        ],
        out_shape=[
            jax.ShapeDtypeStruct((pairs, 2, stations, beams), jnp.bfloat16),
            jax.ShapeDtypeStruct((groups, 2, stations, beams), jnp.bfloat16),
        ],
        compiler_params=pltpu.CompilerParams(vmem_limit_bytes=16 * MIB),
        cost_estimate=pl.CostEstimate(
            flops=200 * stations * beams, bytes_accessed=4 * (pairs + groups) * stations * beams, transcendentals=0
        ),
        name="turns",
    )(first, delays)


def beam_kernel(step_ref, mid_ref, *refs):
    left, power = refs[-2:]
    *r_refs, out_ref = refs[:-2]
    lanes = r_refs[0].shape[3]
    _, _, beams = step_ref.shape
    half = lanes // 2
    width = 2 * LANES
    pairs = GROUP // 2
    j = pl.program_id(1)

    def lay(k, carry):
        both = [r[g, k].astype(jnp.float32) for r in r_refs for g in range(r.shape[0])]
        both = jnp.concatenate(both, 0).T
        left[k, 0] = both.astype(jnp.bfloat16)
        left[k, 1] = jnp.concatenate([both[half:], -both[:half]], 0).astype(jnp.bfloat16)
        return carry

    @pl.when(j == 0)
    def _():
        lax.fori_loop(0, GROUP, lay, 0, unroll=4)

    def one(k, cos, sin):
        out = jnp.dot(left[k, 0], cos.astype(jnp.bfloat16), preferred_element_type=jnp.float32)
        out = out + jnp.dot(left[k, 1], sin.astype(jnp.bfloat16), preferred_element_type=jnp.float32)
        energy = (out * out).reshape(2 * INTEG, lanes // (2 * INTEG), width)
        return jnp.sum(energy, 0) * (1.0 / INTEG)

    for b in range(beams // width):
        at = slice(b * width, (b + 1) * width)
        cm, sm = mid_ref[0, :, at], mid_ref[1, :, at]
        cj, sj = step_ref[0, :, at], step_ref[1, :, at]
        cc, ss, sc, cs = cm * cj, sm * sj, sm * cj, cm * sj
        power[pairs + j, :, at] = one(pairs + j, cc - ss, sc + cs)
        power[pairs - 1 - j, :, at] = one(pairs - 1 - j, cc + ss, sc - cs)
    mine = beams // out_ref.shape[0]
    whole, rest, part, share = packing(mine)

    @pl.when(j == pairs - 1)
    def _():
        for g in range(out_ref.shape[0]):
            own = power[:, :, g * mine : (g + 1) * mine]
            for t in range(whole):
                out_ref[g, t * GROUP : (t + 1) * GROUP] = own[:, :, t * LANES : (t + 1) * LANES].astype(jnp.bfloat16)
            if rest:
                tail = own[:, :, whole * LANES :]
                if part > rest:
                    tail = jnp.concatenate([tail, jnp.zeros((*tail.shape[:2], part - rest), tail.dtype)], 2)
                tail = jnp.concatenate([tail[m * share : (m + 1) * share] for m in range(LANES // part)], 2)
                out_ref[g, whole * GROUP :] = tail.astype(jnp.bfloat16)


def beams_of(steps, mids, received, owners, start, count):
    pairs, _, stations, beams = steps.shape
    lanes = received[0][0].shape[3]
    powers = lanes // (2 * INTEG)
    whole, _, _, share = packing(beams // owners)
    rows = whole * GROUP + share
    return pl.pallas_call(
        beam_kernel,
        grid=(count, pairs),
        in_specs=[
            pl.BlockSpec((None, 2, stations, beams), lambda i, j: (j, 0, 0, 0)),
            pl.BlockSpec((None, 2, stations, beams), lambda i, j: (i + start, 0, 0, 0)),
            *[
                pl.BlockSpec((r.shape[0], GROUP, r.shape[2], lanes), lambda i, j, at=at: (0, i + start - at, 0, 0))
                for r, at in received
            ],
        ],
        out_specs=pl.BlockSpec((owners, None, rows, powers, LANES), lambda i, j: (0, i, 0, 0, 0)),
        out_shape=jax.ShapeDtypeStruct((owners, count, rows, powers, LANES), jnp.bfloat16),
        scratch_shapes=[
            pltpu.VMEM((GROUP, 2, lanes, stations), jnp.bfloat16),
            pltpu.VMEM((GROUP, powers, beams), jnp.float32),
        ],
        compiler_params=pltpu.CompilerParams(vmem_limit_bytes=24 * MIB),
        cost_estimate=pl.CostEstimate(
            flops=8 * count * GROUP * beams * stations * lanes, bytes_accessed=4 * stations * beams, transcendentals=0
        ),
        name="beams",
    )(steps, mids, *[r for r, _ in received])


def tree_kernel(beams, moves_ref, own_ref, next_ref, *refs):

    out_ref, ping, pong = refs[-3:]
    sources, _, _, length, _ = own_ref.shape
    own_ref, next_ref = own_ref.at[:, 0], next_ref.at[:, 0]
    tiles, slots, depth, _ = ping.shape
    span = 2 * length
    whole, rest, part, share = packing(beams)
    for ref, at in ((own_ref, 0), (next_ref, length)):
        for s in range(sources):
            for t in range(whole):
                block = ref[s, t * GROUP : (t + 1) * GROUP].astype(jnp.float32)
                ping[t, s * GROUP : (s + 1) * GROUP, pl.ds(at, length), :] = block
            if rest:
                block = ref[s, whole * GROUP :].astype(jnp.float32)
                for m in range(LANES // part):
                    low = s * GROUP + m * share
                    moved = pltpu.roll(block, LANES - m * part, 2) if m else block
                    ping[whole, low : low + share, pl.ds(at, length), :] = moved
    src, dst = ping, pong
    for level in range(LEVELS):
        h = 2**level
        rows = span if level < LEVELS - 1 else length

        def tree(t, carry, src=src, dst=dst, h=h, rows=rows, level=level):
            start = t * GROUP
            for i in range(GROUP // 2):
                lead = start + i // h * 2 * h + i % h
                masks = []
                for r in range(2):
                    amount = jnp.broadcast_to(moves_ref[level, pl.ds(start + 2 * i + r, 1), :], (rows, LANES))
                    masks.append([amount == by for by in range(SHIFT_MOST)])
                for tile in range(tiles):
                    first = src[tile, lead, pl.ds(0, rows), :]
                    shifted = [src[tile, lead + h, pl.ds(by, rows), :] for by in range(SHIFT_MOST + 1)]
                    for r in range(2):
                        moved = shifted[SHIFT_MOST]
                        for by in range(SHIFT_MOST):
                            moved = jnp.where(masks[r][by], shifted[by], moved)
                        dst[tile, start + 2 * i + r, pl.ds(0, rows), :] = first + moved
            return carry

        lax.fori_loop(0, slots // GROUP, tree, 0)
        src, dst = dst, src
    for tile in range(tiles):
        flat = src.at[tile].reshape(slots * depth, LANES)
        here = min(LANES, beams - tile * LANES)
        for t in range(length):
            turned = (flat[pl.ds(t, slots, stride=depth), :] * 0.5**LEVELS).T
            out_ref[pl.ds(tile * LANES * length + t, here, stride=length), :] = turned[:here]


def dedisperse(moves, own, after, beams, first_slot, total, so_far):
    sources, groups, rows, length, _ = own.shape
    block = LANES // GROUP
    blocks = sources // block
    tiles = pl.cdiv(beams, LANES)
    depth = 2 * length + ROWS
    earlier = [] if so_far is None else [so_far]
    return pl.pallas_call(
        functools.partial(tree_kernel, beams),
        grid=(groups, blocks),
        in_specs=[
            pl.BlockSpec((LEVELS, LANES, LANES), lambda a, i: (0, first_slot // LANES + a * blocks + i, 0)),
            pl.BlockSpec((block, 1, rows, length, LANES), lambda a, i: (i, a, 0, 0, 0)),
            pl.BlockSpec((block, 1, rows, length, LANES), lambda a, i: (i, a, 0, 0, 0)),
            *[pl.BlockSpec(memory_space=pl.ANY) for _ in earlier],
        ],
        out_specs=pl.BlockSpec((beams * length, LANES), lambda a, i: (0, first_slot // LANES + a * blocks + i)),
        out_shape=jax.ShapeDtypeStruct((beams * length, total), jnp.float32),
        scratch_shapes=[pltpu.VMEM((tiles, LANES, depth, LANES), jnp.float32)] * 2,
        input_output_aliases={3: 0} if earlier else {},
        compiler_params=pltpu.CompilerParams(vmem_limit_bytes=16 * MIB),
        cost_estimate=pl.CostEstimate(
            flops=16 * beams * length * GROUP * sources * groups, bytes_accessed=10 * beams * length * GROUP * sources * groups, transcendentals=0
        ),
        name="dedisperse",
    )(moves, own, after, *earlier)


def swapped(x, owners):
    return lax.all_to_all(x.reshape(owners, -1, LANES), "grp", split_axis=0, concat_axis=0, tiled=True)


def local(voltages, filter_taps, delays, shifts):
    owners = lax.axis_size("grp")
    share = voltages.shape[1]
    groups = CHANNELS // (owners * GROUP)
    length = voltages.shape[2] // TRANSFORM // INTEG
    beams = delays.shape[1] // owners
    rim = voltages.shape[2] - (TAPS - 1) * TRANSFORM
    cuts = [0, ROWS, share] if share > ROWS else [0, share]
    early = [groups // 2, groups - groups // 2] if groups > 1 else [groups]
    calls = [groups // 2] + [1] * (groups - groups // 2) if groups > 1 else [groups]
    moves = jnp.broadcast_to(shifts[:, :, None], (*shifts.shape, LANES))
    halos = []
    for first, last in zip(cuts, cuts[1:]):
        halos.append(shift_along(voltages[:, first:last, rim:], "tm", 1))
    received = []
    for n, (first, last) in enumerate(zip(cuts, cuts[1:])):
        pieces = early if last == share else [groups]
        arrays = channelize(voltages, halos[n], filter_taps, owners, first, last, pieces)
        start = 0
        for many, array in zip(pieces, arrays):
            here = swapped(array, owners)
            here = here.reshape(owners, many * GROUP, last - first, LANES)
            if (last - first) % ROWS:
                here = jnp.transpose(here, (1, 0, 2, 3)).reshape(1, many * GROUP, -1, LANES)
            received.append((here, start, start + many))
            start += many
    by_owner = delays.reshape(owners, share, delays.shape[1])
    delays = jnp.concatenate([by_owner[:, a:b].reshape(-1, delays.shape[1]) for a, b in zip(cuts, cuts[1:])])
    mine = (lax.axis_index("grp") * GROUP).astype(jnp.int32).reshape(1)
    steps, mids = turns(mine, delays, owners, groups)
    out, start = None, 0
    for many in calls:
        arrays = [(r, low) for r, low, high in received if low <= start and start + many <= high]
        power = beams_of(steps, mids, arrays, owners, start, many)
        owned = swapped(power, owners).reshape(power.shape)
        after = shift_along(owned, "tm", -1)
        out = dedisperse(moves, owned, after, beams, start * owners * GROUP, CHANNELS, out)
        start += many
    return jnp.transpose(out.reshape(beams, length, CHANNELS), (0, 2, 1))


def solution(mesh):
    placed = (P(None, "grp", "tm"), P(), P(), P())
    return jax.shard_map(local, mesh=mesh, in_specs=placed, out_specs=P("grp", None, "tm"), check_vma=False)
```

```python
import functools
import math

import jax
import jax.numpy as jnp
import numpy as np
from jax import lax
from jax.experimental import pallas as pl
from jax.experimental.pallas import tpu as pltpu
from jax.sharding import PartitionSpec as P

TRANSFORM = 4096
CHANNELS = 512
TAPS = 4
INTEG = 8
LEVELS = 4
SHIFT_MOST = 2

RADIX = 4
SUB = TRANSFORM // RADIX
PER = CHANNELS // RADIX
LANES = 128
WIDE = 2 * LANES
ROWS = 8
STEPS = 2
GROUP = 2**LEVELS
MIB = 1024 * 1024


def shift_along(x, axis, by):
    length = lax.axis_size(axis)
    pairs = [(i, i + by) for i in range(length) if 0 <= i + by < length]
    return lax.ppermute(x, axis, pairs)


def table_factors():
    k = (RADIX * np.arange(PER)[None, :] + np.arange(RADIX)[:, None])[:, None, :]
    fine = k * np.arange(ROWS)[None, :, None] % TRANSFORM
    coarse = k * (ROWS * np.arange(SUB // ROWS))[None, :, None] % TRANSFORM
    turn = 2.0 * np.pi / TRANSFORM
    scale = 1.0 / math.sqrt(TRANSFORM)
    fine = np.stack([np.cos(fine * turn), np.sin(fine * turn)], 1)
    coarse = np.stack([np.cos(coarse * turn), np.sin(coarse * turn)], 1) * scale
    return fine.astype(np.float32), coarse.astype(np.float32)


def channel_kernel(frames, x_ref, halo_ref, taps_ref, fine_ref, coarse_ref, *refs):
    *out_refs, table, folded, spectra, turned, weights, rim = refs
    stations = x_ref.shape[1]
    here = x_ref.shape[2] // TRANSFORM
    step, steps = pl.program_id(1), pl.num_programs(1)

    @pl.when((pl.program_id(0) == 0) & (step == 0))
    def _():
        for p in range(TAPS):
            weights[p] = jnp.broadcast_to(taps_ref[p : p + 1, :], (ROWS, TRANSFORM)).astype(jnp.bfloat16)

        def build(u, carry):
            for q in range(RADIX):
                ca, sa = fine_ref[q, 0], fine_ref[q, 1]
                cs, ss = [], []
                for half in range(2):
                    cb = coarse_ref[q, 0, pl.ds(2 * u + half, 1), :]
                    sb = coarse_ref[q, 1, pl.ds(2 * u + half, 1), :]
                    cs.append(cb * ca - sb * sa)
                    ss.append(sb * ca + cb * sa)
                c = jnp.concatenate(cs, 0).astype(jnp.bfloat16)
                s = jnp.concatenate(ss, 0)
                top = pl.ds(pl.multiple_of(u * 2 * ROWS, 2 * ROWS), 2 * ROWS)
                low = pl.ds(pl.multiple_of(SUB + u * 2 * ROWS, 2 * ROWS), 2 * ROWS)
                table[q, top, :PER] = c
                table[q, top, PER:] = (-s).astype(jnp.bfloat16)
                table[q, low, :PER] = s.astype(jnp.bfloat16)
                table[q, low, PER:] = c
            return carry

        lax.fori_loop(0, SUB // (2 * ROWS), build, 0)

    @pl.when(step == 0)
    def _():
        rim[...] = halo_ref[...]

    def full(x):
        if stations < ROWS:
            x = jnp.concatenate([x, jnp.zeros((ROWS - stations, WIDE), x.dtype)], 0)
        return x

    parts = [(c, j) for c in range(2) for j in range(RADIX)]

    def columns(tile, carry):
        taps = [
            [weights[p, :, pl.ds(pl.multiple_of(j * SUB + tile * WIDE, WIDE), WIDE)] for j in range(RADIX)]
            for p in range(TAPS)
        ]

        def at(ref, f, c, j):
            start = pl.multiple_of(f * TRANSFORM + j * SUB + tile * WIDE, WIDE)
            return full(ref[c, :, pl.ds(start, WIDE)])

        def filtered(f, before):
            z, after = {}, []
            for (c, j), old in zip(parts, before):
                now = at(x_ref, f, c, j)
                total = taps[0][j] * now
                for p in range(1, TAPS):
                    total = total + taps[p][j] * old[p - 1]
                z[c, j] = total
                after.append((now, *old[:-1]))
            even = [z[c, 0] + z[c, 2] for c in range(2)]
            odd = [z[c, 0] - z[c, 2] for c in range(2)]
            even1 = [z[c, 1] + z[c, 3] for c in range(2)]
            odd1 = [z[c, 1] - z[c, 3] for c in range(2)]
            y = {
                (0, 0): even[0] + even1[0], (0, 1): even[1] + even1[1],
                (2, 0): even[0] - even1[0], (2, 1): even[1] - even1[1],
                (1, 0): odd[0] + odd1[1], (1, 1): odd[1] - odd1[0],
                (3, 0): odd[0] - odd1[1], (3, 1): odd[1] + odd1[0],
            }
            return y, after

        def pair(two, before):
            f = two * 2
            first, before = filtered(f, before)
            second, before = filtered(f + 1, before)
            rows = pl.ds(pl.multiple_of((step * here + f) * ROWS, 2 * ROWS), 2 * ROWS)
            for q in range(RADIX):
                for c in range(2):
                    both = jnp.concatenate([first[q, c], second[q, c]], 0)
                    lanes = pl.ds(pl.multiple_of(c * SUB + tile * WIDE, WIDE), WIDE)
                    folded[q, rows, lanes] = both.astype(jnp.bfloat16)
            return before

        before = [tuple(at(rim, TAPS - 2 - p, c, j) for p in range(TAPS - 1)) for c, j in parts]
        lax.fori_loop(0, here // 2, pair, before)
        return carry

    lax.fori_loop(0, SUB // WIDE, columns, 0)

    @pl.when(step < steps - 1)
    def _():
        rim[...] = x_ref[:, :, pl.ds((here - TAPS + 1) * TRANSFORM, (TAPS - 1) * TRANSFORM)]

    def transform(q):
        both = jnp.dot(folded[q], table[q], preferred_element_type=jnp.float32)
        spectra[q % 2, 0] = both[:, :PER]
        spectra[q % 2, 1] = both[:, PER:]

    def lay(q):
        powers = frames // INTEG
        for s in range(stations):
            rows = [
                spectra[q % 2, part, pl.ds(i * ROWS + s, powers, stride=INTEG * ROWS), :]
                for part in range(2)
                for i in range(INTEG)
            ]
            turned[q % 2, pl.ds(s, PER, stride=ROWS), :] = jnp.concatenate(rows, 0).T
        start = 0
        for out_ref in out_refs:
            owners, groups, per = out_ref.shape[:3]
            for n in range(groups):
                many = owners * per * ROWS
                block = turned[q % 2, start : start + many].reshape(owners, per, ROWS, LANES)
                out_ref[:, n, :, q] = block[:, :, :stations].astype(jnp.bfloat16)
                start += many

    @pl.when(step == steps - 1)
    def _():
        for q in range(RADIX + 1):
            if q < RADIX:
                transform(q)
            if q:
                lay(q - 1)


def channelize(voltages, halo, filter_taps, owners, first, last, pieces):
    stations = last - first
    frames = voltages.shape[2] // TRANSFORM
    block = ROWS if stations % ROWS == 0 else stations
    assert block <= ROWS and 2 * frames == LANES and first % block == 0
    offset = first // block
    per = GROUP // RADIX
    fine, coarse = table_factors()
    return pl.pallas_call(
        functools.partial(channel_kernel, frames),
        grid=(stations // block, STEPS),
        in_specs=[
            pl.BlockSpec((2, block, voltages.shape[2] // STEPS), lambda i, h: (0, i + offset, h)),
            pl.BlockSpec((2, block, halo.shape[2]), lambda i, h: (0, i, 0)),
            pl.BlockSpec(filter_taps.shape, lambda i, h: (0, 0)),
            pl.BlockSpec(fine.shape, lambda i, h: (0, 0, 0, 0)),
            pl.BlockSpec(coarse.shape, lambda i, h: (0, 0, 0, 0)),
        ],
        out_specs=[
            pl.BlockSpec((owners, n, per, RADIX, block, LANES), lambda i, h: (0, 0, 0, 0, i, 0)) for n in pieces
        ],
        out_shape=[
            jax.ShapeDtypeStruct((owners, n, per, RADIX, stations, LANES), jnp.bfloat16) for n in pieces
        ],
        scratch_shapes=[
            pltpu.VMEM((RADIX, 2 * SUB, 2 * PER), jnp.bfloat16),
            pltpu.VMEM((RADIX, frames * ROWS, 2 * SUB), jnp.bfloat16),
            pltpu.VMEM((2, 2, frames * ROWS, PER), jnp.float32),
            pltpu.VMEM((2, PER * ROWS, LANES), jnp.float32),
            pltpu.VMEM((TAPS, ROWS, TRANSFORM), jnp.bfloat16),
            pltpu.VMEM((2, block, (TAPS - 1) * TRANSFORM), jnp.bfloat16),
        ],
        compiler_params=pltpu.CompilerParams(vmem_limit_bytes=40 * MIB),
        cost_estimate=pl.CostEstimate(
            flops=stations * frames * 8 * SUB * CHANNELS, bytes_accessed=stations * 4 * voltages.shape[2], transcendentals=0
        ),
        name="channelize",
    )(voltages, halo, filter_taps, jnp.asarray(fine), jnp.asarray(coarse))


def turn_of(steps):
    whole = 2 * TRANSFORM
    quarter = whole // 4
    moved = (steps & (whole - 1)) + quarter // 2
    x = ((moved & (quarter - 1)) - quarter // 2).astype(jnp.float32) * (2.0 * math.pi / whole)
    side = (moved >> (quarter.bit_length() - 1)) & 3
    y = x * x
    s = x * (1.0 + y * (-1.0 / 6 + y * (1.0 / 120 + y * (-1.0 / 5040 + y * (1.0 / 362880)))))
    c = 1.0 + y * (-0.5 + y * (1.0 / 24 + y * (-1.0 / 720 + y * (1.0 / 40320))))
    odd = (side & 1) == 1
    cos = jnp.where(odd, s, c)
    sin = jnp.where(odd, c, s)
    cos = jnp.where((side == 1) | (side == 2), -cos, cos)
    sin = jnp.where(side >= 2, -sin, sin)
    return cos, sin


def packing(mine):
    whole, rest = divmod(mine, LANES)
    part = 1 << (rest - 1).bit_length() if rest else LANES
    share = part * GROUP // LANES if rest else 0
    return whole, rest, part, share


def turns(first, delays, owners, groups):
    stations, beams = delays.shape
    pairs = GROUP // 2

    def kernel(first_ref, delays_ref, step_ref, mid_ref):
        ch, sh = turn_of(delays_ref[...])
        twice = 2.0 * (ch * ch - sh * sh)
        before, now = (ch, -sh), (ch, sh)
        for j in range(pairs):
            step_ref[j, 0] = now[0].astype(jnp.bfloat16)
            step_ref[j, 1] = now[1].astype(jnp.bfloat16)
            before, now = now, (twice * now[0] - before[0], twice * now[1] - before[1])
        for a in range(groups):
            c, s = turn_of(delays_ref[...] * (2 * (first_ref[0] + owners * GROUP * a) + GROUP - 1))
            mid_ref[a, 0] = (c * (1.0 / math.sqrt(stations))).astype(jnp.bfloat16)
            mid_ref[a, 1] = (s * (1.0 / math.sqrt(stations))).astype(jnp.bfloat16)

    return pl.pallas_call(
        kernel,
        grid=(stations // (2 * ROWS),),
        in_specs=[
            pl.BlockSpec(memory_space=pltpu.SMEM),
            pl.BlockSpec((2 * ROWS, beams), lambda i: (i, 0)),
        ],
        out_specs=[
            pl.BlockSpec((pairs, 2, 2 * ROWS, beams), lambda i: (0, 0, i, 0)),
            pl.BlockSpec((groups, 2, 2 * ROWS, beams), lambda i: (0, 0, i, 0)),
        ],
        out_shape=[
            jax.ShapeDtypeStruct((pairs, 2, stations, beams), jnp.bfloat16),
            jax.ShapeDtypeStruct((groups, 2, stations, beams), jnp.bfloat16),
        ],
        compiler_params=pltpu.CompilerParams(vmem_limit_bytes=16 * MIB),
        cost_estimate=pl.CostEstimate(
            flops=200 * stations * beams, bytes_accessed=4 * (pairs + groups) * stations * beams, transcendentals=0
        ),
        name="turns",
    )(first, delays)


def beam_kernel(apart, step_ref, mid_ref, *refs):
    left, power = refs[-2:]
    r_refs, out_refs = refs[: -2 - apart], refs[-2 - apart : -2]
    lanes = r_refs[0].shape[3]
    _, _, beams = step_ref.shape
    half = lanes // 2
    width = 2 * LANES
    pairs = GROUP // 2
    j = pl.program_id(1)

    def lay(k, carry):
        both = [r[g, k].astype(jnp.float32) for r in r_refs for g in range(r.shape[0])]
        both = jnp.concatenate(both, 0).T
        left[k, 0] = both.astype(jnp.bfloat16)
        left[k, 1] = jnp.concatenate([both[half:], -both[:half]], 0).astype(jnp.bfloat16)
        return carry

    @pl.when(j == 0)
    def _():
        lax.fori_loop(0, GROUP, lay, 0, unroll=4)

    def one(k, cos, sin):
        out = jnp.dot(left[k, 0], cos.astype(jnp.bfloat16), preferred_element_type=jnp.float32)
        out = out + jnp.dot(left[k, 1], sin.astype(jnp.bfloat16), preferred_element_type=jnp.float32)
        energy = (out * out).reshape(2 * INTEG, lanes // (2 * INTEG), width)
        return jnp.sum(energy, 0) * (1.0 / INTEG)

    for b in range(beams // width):
        at = slice(b * width, (b + 1) * width)
        cm, sm = mid_ref[0, :, at], mid_ref[1, :, at]
        cj, sj = step_ref[0, :, at], step_ref[1, :, at]
        cc, ss, sc, cs = cm * cj, sm * sj, sm * cj, cm * sj
        power[pairs + j, :, at] = one(pairs + j, cc - ss, sc + cs)
        power[pairs - 1 - j, :, at] = one(pairs - 1 - j, cc + ss, sc - cs)
    mine = beams // out_refs[0].shape[0]
    whole, rest, part, share = packing(mine)

    def give(out_ref):
        for g in range(out_ref.shape[0]):
            own = power[:, :, g * mine : (g + 1) * mine]
            for t in range(whole):
                out_ref[g, t * GROUP : (t + 1) * GROUP] = own[:, :, t * LANES : (t + 1) * LANES].astype(jnp.bfloat16)
            if rest:
                tail = own[:, :, whole * LANES :]
                if part > rest:
                    tail = jnp.concatenate([tail, jnp.zeros((*tail.shape[:2], part - rest), tail.dtype)], 2)
                tail = jnp.concatenate([tail[m * share : (m + 1) * share] for m in range(LANES // part)], 2)
                out_ref[g, whole * GROUP :] = tail.astype(jnp.bfloat16)

    for n, out_ref in enumerate(out_refs):
        mine_now = (pl.program_id(0) == n) | (apart == 1)
        pl.when(mine_now & (j == pairs - 1))(functools.partial(give, out_ref))


def beams_of(steps, mids, received, owners, start, count, apart):
    pairs, _, stations, beams = steps.shape
    lanes = received[0][0].shape[3]
    powers = lanes // (2 * INTEG)
    whole, _, _, share = packing(beams // owners)
    rows = whole * GROUP + share
    held = count // apart
    return pl.pallas_call(
        functools.partial(beam_kernel, apart),
        grid=(count, pairs),
        in_specs=[
            pl.BlockSpec((None, 2, stations, beams), lambda i, j: (j, 0, 0, 0)),
            pl.BlockSpec((None, 2, stations, beams), lambda i, j: (i + start, 0, 0, 0)),
            *[
                pl.BlockSpec((r.shape[0], GROUP, r.shape[2], lanes), lambda i, j, at=at: (0, i + start - at, 0, 0))
                for r, at in received
            ],
        ],
        out_specs=[
            pl.BlockSpec((owners, None, rows, powers, LANES), lambda i, j: (0, i if apart == 1 else 0, 0, 0, 0))
        ] * apart,
        out_shape=[jax.ShapeDtypeStruct((owners, held, rows, powers, LANES), jnp.bfloat16)] * apart,
        scratch_shapes=[
            pltpu.VMEM((GROUP, 2, lanes, stations), jnp.bfloat16),
            pltpu.VMEM((GROUP, powers, beams), jnp.float32),
        ],
        compiler_params=pltpu.CompilerParams(vmem_limit_bytes=24 * MIB),
        cost_estimate=pl.CostEstimate(
            flops=8 * count * GROUP * beams * stations * lanes, bytes_accessed=4 * stations * beams, transcendentals=0
        ),
        name="beams",
    )(steps, mids, *[r for r, _ in received])


def tree_kernel(beams, moves_ref, own_ref, next_ref, *refs):

    out_ref, ping, pong = refs[-3:]
    sources, _, _, length, _ = own_ref.shape
    own_ref, next_ref = own_ref.at[:, 0], next_ref.at[:, 0]
    tiles, slots, depth, _ = ping.shape
    span = 2 * length
    whole, rest, part, share = packing(beams)
    for ref, at in ((own_ref, 0), (next_ref, length)):
        for s in range(sources):
            for t in range(whole):
                block = ref[s, t * GROUP : (t + 1) * GROUP].astype(jnp.float32)
                ping[t, s * GROUP : (s + 1) * GROUP, pl.ds(at, length), :] = block
            if rest:
                block = ref[s, whole * GROUP :].astype(jnp.float32)
                for m in range(LANES // part):
                    low = s * GROUP + m * share
                    moved = pltpu.roll(block, LANES - m * part, 2) if m else block
                    ping[whole, low : low + share, pl.ds(at, length), :] = moved
    src, dst = ping, pong
    for level in range(LEVELS):
        h = 2**level
        rows = span if level < LEVELS - 1 else length

        def tree(t, carry, src=src, dst=dst, h=h, rows=rows, level=level):
            start = t * GROUP
            for i in range(GROUP // 2):
                lead = start + i // h * 2 * h + i % h
                masks = []
                for r in range(2):
                    amount = jnp.broadcast_to(moves_ref[level, pl.ds(start + 2 * i + r, 1), :], (rows, LANES))
                    masks.append([amount == by for by in range(SHIFT_MOST)])
                for tile in range(tiles):
                    first = src[tile, lead, pl.ds(0, rows), :]
                    shifted = [src[tile, lead + h, pl.ds(by, rows), :] for by in range(SHIFT_MOST + 1)]
                    for r in range(2):
                        moved = shifted[SHIFT_MOST]
                        for by in range(SHIFT_MOST):
                            moved = jnp.where(masks[r][by], shifted[by], moved)
                        dst[tile, start + 2 * i + r, pl.ds(0, rows), :] = first + moved
            return carry

        lax.fori_loop(0, slots // GROUP, tree, 0)
        src, dst = dst, src
    for tile in range(tiles):
        flat = src.at[tile].reshape(slots * depth, LANES)
        here = min(LANES, beams - tile * LANES)
        for t in range(length):
            turned = (flat[pl.ds(t, slots, stride=depth), :] * 0.5**LEVELS).T
            out_ref[pl.ds(tile * LANES * length + t, here, stride=length), :] = turned[:here]


def dedisperse(moves, own, after, beams, first_slot, total, so_far):
    sources, groups, rows, length, _ = own.shape
    block = LANES // GROUP
    blocks = sources // block
    tiles = pl.cdiv(beams, LANES)
    depth = 2 * length + ROWS
    earlier = [] if so_far is None else [so_far]
    return pl.pallas_call(
        functools.partial(tree_kernel, beams),
        grid=(groups, blocks),
        in_specs=[
            pl.BlockSpec((LEVELS, LANES, LANES), lambda a, i: (0, first_slot // LANES + a * blocks + i, 0)),
            pl.BlockSpec((block, 1, rows, length, LANES), lambda a, i: (i, a, 0, 0, 0)),
            pl.BlockSpec((block, 1, rows, length, LANES), lambda a, i: (i, a, 0, 0, 0)),
            *[pl.BlockSpec(memory_space=pl.ANY) for _ in earlier],
        ],
        out_specs=pl.BlockSpec((beams * length, LANES), lambda a, i: (0, first_slot // LANES + a * blocks + i)),
        out_shape=jax.ShapeDtypeStruct((beams * length, total), jnp.float32),
        scratch_shapes=[pltpu.VMEM((tiles, LANES, depth, LANES), jnp.float32)] * 2,
        input_output_aliases={3: 0} if earlier else {},
        compiler_params=pltpu.CompilerParams(vmem_limit_bytes=16 * MIB),
        cost_estimate=pl.CostEstimate(
            flops=16 * beams * length * GROUP * sources * groups, bytes_accessed=10 * beams * length * GROUP * sources * groups, transcendentals=0
        ),
        name="dedisperse",
    )(moves, own, after, *earlier)


def swapped(x, owners):
    return lax.all_to_all(x.reshape(owners, -1, LANES), "grp", split_axis=0, concat_axis=0, tiled=True)


def local(voltages, filter_taps, delays, shifts):
    owners = lax.axis_size("grp")
    share = voltages.shape[1]
    groups = CHANNELS // (owners * GROUP)
    length = voltages.shape[2] // TRANSFORM // INTEG
    beams = delays.shape[1] // owners
    rim = voltages.shape[2] - (TAPS - 1) * TRANSFORM
    cuts = [0, ROWS, share] if share > ROWS else [0, share]
    early = [groups // 2, groups - groups // 2] if groups > 1 else [groups]
    moves = jnp.broadcast_to(shifts[:, :, None], (*shifts.shape, LANES))
    halos = []
    for n, (first, last) in enumerate(zip(cuts, cuts[1:])):
        halos.append(shift_along(voltages[:, first:last, rim:], "tm", 1))
    received = []
    for n, (first, last) in enumerate(zip(cuts, cuts[1:])):
        pieces = early if last == share else [groups]
        arrays = channelize(voltages, halos[n], filter_taps, owners, first, last, pieces)
        start = 0
        for many, array in zip(pieces, arrays):
            here = swapped(array, owners)
            here = here.reshape(owners, many * GROUP, last - first, LANES)
            if (last - first) % ROWS:
                here = jnp.transpose(here, (1, 0, 2, 3)).reshape(1, many * GROUP, -1, LANES)
            received.append((here, start, start + many))
            start += many
    by_owner = delays.reshape(owners, share, delays.shape[1])
    delays = jnp.concatenate([by_owner[:, a:b].reshape(-1, delays.shape[1]) for a, b in zip(cuts, cuts[1:])])
    mine = (lax.axis_index("grp") * GROUP).astype(jnp.int32).reshape(1)
    steps, mids = turns(mine, delays, owners, groups)
    out, start, n = None, 0, 0
    for call, many in enumerate(early):
        arrays = [(r, low) for r, low, high in received if low <= start and start + many <= high]
        apart = many if call else 1
        given = beams_of(steps, mids, arrays, owners, start, many, apart)
        for power in given:
            owned = swapped(power, owners).reshape(power.shape)
            after = shift_along(owned, "tm", -1)
            out = dedisperse(moves, owned, after, beams, start * owners * GROUP, CHANNELS, out)
            start += many // apart
            n += 1
    return jnp.transpose(out.reshape(beams, length, CHANNELS), (0, 2, 1))


def solution(mesh):
    placed = (P(None, "grp", "tm"), P(), P(), P())
    return jax.shard_map(local, mesh=mesh, in_specs=placed, out_specs=P("grp", None, "tm"), check_vma=False)
```

```python
import functools
import math

import jax
import jax.numpy as jnp
import numpy as np
from jax import lax
from jax.experimental import pallas as pl
from jax.experimental.pallas import tpu as pltpu
from jax.sharding import PartitionSpec as P

TRANSFORM = 4096
CHANNELS = 512
TAPS = 4
INTEG = 8
LEVELS = 4
SHIFT_MOST = 2

RADIX = 4
SUB = TRANSFORM // RADIX
PER = CHANNELS // RADIX
LANES = 128
WIDE = 2 * LANES
ROWS = 8
STEPS = 2
GROUP = 2**LEVELS
MIB = 1024 * 1024


def shift_along(x, axis, by):
    length = lax.axis_size(axis)
    pairs = [(i, i + by) for i in range(length) if 0 <= i + by < length]
    return lax.ppermute(x, axis, pairs)


def table_factors():
    k = (RADIX * np.arange(PER)[None, :] + np.arange(RADIX)[:, None])[:, None, :]
    fine = k * np.arange(ROWS)[None, :, None] % TRANSFORM
    coarse = k * (ROWS * np.arange(SUB // ROWS))[None, :, None] % TRANSFORM
    turn = 2.0 * np.pi / TRANSFORM
    scale = 1.0 / math.sqrt(TRANSFORM)
    fine = np.stack([np.cos(fine * turn), np.sin(fine * turn)], 1)
    coarse = np.stack([np.cos(coarse * turn), np.sin(coarse * turn)], 1) * scale
    return fine.astype(np.float32), coarse.astype(np.float32)


def channel_kernel(frames, x_ref, halo_ref, taps_ref, fine_ref, coarse_ref, *refs):
    *out_refs, table, folded, spectra, turned, weights, rim = refs
    stations = x_ref.shape[1]
    here = x_ref.shape[2] // TRANSFORM
    step, steps = pl.program_id(1), pl.num_programs(1)

    @pl.when((pl.program_id(0) == 0) & (step == 0))
    def _():
        for p in range(TAPS):
            weights[p] = jnp.broadcast_to(taps_ref[p : p + 1, :], (ROWS, TRANSFORM)).astype(jnp.bfloat16)

        def build(u, carry):
            for q in range(RADIX):
                ca, sa = fine_ref[q, 0], fine_ref[q, 1]
                cs, ss = [], []
                for half in range(2):
                    cb = coarse_ref[q, 0, pl.ds(2 * u + half, 1), :]
                    sb = coarse_ref[q, 1, pl.ds(2 * u + half, 1), :]
                    cs.append(cb * ca - sb * sa)
                    ss.append(sb * ca + cb * sa)
                c = jnp.concatenate(cs, 0).astype(jnp.bfloat16)
                s = jnp.concatenate(ss, 0)
                top = pl.ds(pl.multiple_of(u * 2 * ROWS, 2 * ROWS), 2 * ROWS)
                low = pl.ds(pl.multiple_of(SUB + u * 2 * ROWS, 2 * ROWS), 2 * ROWS)
                table[q, top, :PER] = c
                table[q, top, PER:] = (-s).astype(jnp.bfloat16)
                table[q, low, :PER] = s.astype(jnp.bfloat16)
                table[q, low, PER:] = c
            return carry

        lax.fori_loop(0, SUB // (2 * ROWS), build, 0)

    @pl.when(step == 0)
    def _():
        rim[...] = halo_ref[...]

    def full(x):
        if stations < ROWS:
            x = jnp.concatenate([x, jnp.zeros((ROWS - stations, WIDE), x.dtype)], 0)
        return x

    parts = [(c, j) for c in range(2) for j in range(RADIX)]

    def columns(tile, carry):
        taps = [
            [weights[p, :, pl.ds(pl.multiple_of(j * SUB + tile * WIDE, WIDE), WIDE)] for j in range(RADIX)]
            for p in range(TAPS)
        ]

        def at(ref, f, c, j):
            start = pl.multiple_of(f * TRANSFORM + j * SUB + tile * WIDE, WIDE)
            return full(ref[c, :, pl.ds(start, WIDE)])

        def filtered(f, before):
            z, after = {}, []
            for (c, j), old in zip(parts, before):
                now = at(x_ref, f, c, j)
                total = taps[0][j] * now
                for p in range(1, TAPS):
                    total = total + taps[p][j] * old[p - 1]
                z[c, j] = total
                after.append((now, *old[:-1]))
            even = [z[c, 0] + z[c, 2] for c in range(2)]
            odd = [z[c, 0] - z[c, 2] for c in range(2)]
            even1 = [z[c, 1] + z[c, 3] for c in range(2)]
            odd1 = [z[c, 1] - z[c, 3] for c in range(2)]
            y = {
                (0, 0): even[0] + even1[0], (0, 1): even[1] + even1[1],
                (2, 0): even[0] - even1[0], (2, 1): even[1] - even1[1],
                (1, 0): odd[0] + odd1[1], (1, 1): odd[1] - odd1[0],
                (3, 0): odd[0] - odd1[1], (3, 1): odd[1] + odd1[0],
            }
            return y, after

        def pair(two, before):
            f = two * 2
            first, before = filtered(f, before)
            second, before = filtered(f + 1, before)
            rows = pl.ds(pl.multiple_of((step * here + f) * ROWS, 2 * ROWS), 2 * ROWS)
            for q in range(RADIX):
                for c in range(2):
                    both = jnp.concatenate([first[q, c], second[q, c]], 0)
                    lanes = pl.ds(pl.multiple_of(c * SUB + tile * WIDE, WIDE), WIDE)
                    folded[q, rows, lanes] = both.astype(jnp.bfloat16)
            return before

        before = [tuple(at(rim, TAPS - 2 - p, c, j) for p in range(TAPS - 1)) for c, j in parts]
        lax.fori_loop(0, here // 2, pair, before)
        return carry

    lax.fori_loop(0, SUB // WIDE, columns, 0)

    @pl.when(step < steps - 1)
    def _():
        rim[...] = x_ref[:, :, pl.ds((here - TAPS + 1) * TRANSFORM, (TAPS - 1) * TRANSFORM)]

    def transform(q):
        both = jnp.dot(folded[q], table[q], preferred_element_type=jnp.float32)
        spectra[q % 2, 0] = both[:, :PER]
        spectra[q % 2, 1] = both[:, PER:]

    def lay(q):
        powers = frames // INTEG
        for s in range(stations):
            rows = [
                spectra[q % 2, part, pl.ds(i * ROWS + s, powers, stride=INTEG * ROWS), :]
                for part in range(2)
                for i in range(INTEG)
            ]
            turned[q % 2, pl.ds(s, PER, stride=ROWS), :] = jnp.concatenate(rows, 0).T
        start = 0
        for out_ref in out_refs:
            owners, groups, per = out_ref.shape[:3]
            for n in range(groups):
                many = owners * per * ROWS
                block = turned[q % 2, start : start + many].reshape(owners, per, ROWS, LANES)
                out_ref[:, n, :, q] = block[:, :, :stations].astype(jnp.bfloat16)
                start += many

    @pl.when(step == steps - 1)
    def _():
        for q in range(RADIX + 1):
            if q < RADIX:
                transform(q)
            if q:
                lay(q - 1)


def channelize(voltages, halo, filter_taps, owners, first, last, pieces):
    stations = last - first
    frames = voltages.shape[2] // TRANSFORM
    block = ROWS if stations % ROWS == 0 else stations
    assert block <= ROWS and 2 * frames == LANES and first % block == 0
    offset = first // block
    per = GROUP // RADIX
    fine, coarse = table_factors()
    return pl.pallas_call(
        functools.partial(channel_kernel, frames),
        grid=(stations // block, STEPS),
        in_specs=[
            pl.BlockSpec((2, block, voltages.shape[2] // STEPS), lambda i, h: (0, i + offset, h)),
            pl.BlockSpec((2, block, halo.shape[2]), lambda i, h: (0, i, 0)),
            pl.BlockSpec(filter_taps.shape, lambda i, h: (0, 0)),
            pl.BlockSpec(fine.shape, lambda i, h: (0, 0, 0, 0)),
            pl.BlockSpec(coarse.shape, lambda i, h: (0, 0, 0, 0)),
        ],
        out_specs=[
            pl.BlockSpec((owners, n, per, RADIX, block, LANES), lambda i, h: (0, 0, 0, 0, i, 0)) for n in pieces
        ],
        out_shape=[
            jax.ShapeDtypeStruct((owners, n, per, RADIX, stations, LANES), jnp.bfloat16) for n in pieces
        ],
        scratch_shapes=[
            pltpu.VMEM((RADIX, 2 * SUB, 2 * PER), jnp.bfloat16),
            pltpu.VMEM((RADIX, frames * ROWS, 2 * SUB), jnp.bfloat16),
            pltpu.VMEM((2, 2, frames * ROWS, PER), jnp.float32),
            pltpu.VMEM((2, PER * ROWS, LANES), jnp.float32),
            pltpu.VMEM((TAPS, ROWS, TRANSFORM), jnp.bfloat16),
            pltpu.VMEM((2, block, (TAPS - 1) * TRANSFORM), jnp.bfloat16),
        ],
        compiler_params=pltpu.CompilerParams(vmem_limit_bytes=40 * MIB),
        cost_estimate=pl.CostEstimate(
            flops=stations * frames * 8 * SUB * CHANNELS, bytes_accessed=stations * 4 * voltages.shape[2], transcendentals=0
        ),
        name="channelize",
    )(voltages, halo, filter_taps, jnp.asarray(fine), jnp.asarray(coarse))


def turn_of(steps):
    whole = 2 * TRANSFORM
    quarter = whole // 4
    moved = (steps & (whole - 1)) + quarter // 2
    x = ((moved & (quarter - 1)) - quarter // 2).astype(jnp.float32) * (2.0 * math.pi / whole)
    side = (moved >> (quarter.bit_length() - 1)) & 3
    y = x * x
    s = x * (1.0 + y * (-1.0 / 6 + y * (1.0 / 120 + y * (-1.0 / 5040 + y * (1.0 / 362880)))))
    c = 1.0 + y * (-0.5 + y * (1.0 / 24 + y * (-1.0 / 720 + y * (1.0 / 40320))))
    odd = (side & 1) == 1
    cos = jnp.where(odd, s, c)
    sin = jnp.where(odd, c, s)
    cos = jnp.where((side == 1) | (side == 2), -cos, cos)
    sin = jnp.where(side >= 2, -sin, sin)
    return cos, sin


def packing(mine):
    whole, rest = divmod(mine, LANES)
    part = 1 << (rest - 1).bit_length() if rest else LANES
    share = part * GROUP // LANES if rest else 0
    return whole, rest, part, share


def turns(first, delays, owners, counts):
    stations, beams = delays.shape
    pairs = GROUP // 2

    def kernel(first_ref, delays_ref, step_ref, *mid_refs):
        ch, sh = turn_of(delays_ref[...])
        twice = 2.0 * (ch * ch - sh * sh)
        before, now = (ch, -sh), (ch, sh)
        for j in range(pairs):
            step_ref[j, 0] = now[0].astype(jnp.bfloat16)
            step_ref[j, 1] = now[1].astype(jnp.bfloat16)
            before, now = now, (twice * now[0] - before[0], twice * now[1] - before[1])
        for a, (mid_ref, at) in enumerate((ref, n) for ref in mid_refs for n in range(ref.shape[0])):
            c, s = turn_of(delays_ref[...] * (2 * (first_ref[0] + owners * GROUP * a) + GROUP - 1))
            mid_ref[at, 0] = (c * (1.0 / math.sqrt(stations))).astype(jnp.bfloat16)
            mid_ref[at, 1] = (s * (1.0 / math.sqrt(stations))).astype(jnp.bfloat16)

    return pl.pallas_call(
        kernel,
        grid=(stations // (2 * ROWS),),
        in_specs=[
            pl.BlockSpec(memory_space=pltpu.SMEM),
            pl.BlockSpec((2 * ROWS, beams), lambda i: (i, 0)),
        ],
        out_specs=[
            pl.BlockSpec((pairs, 2, 2 * ROWS, beams), lambda i: (0, 0, i, 0)),
            *[pl.BlockSpec((n, 2, 2 * ROWS, beams), lambda i: (0, 0, i, 0)) for n in counts],
        ],
        out_shape=[
            jax.ShapeDtypeStruct((pairs, 2, stations, beams), jnp.bfloat16),
            *[jax.ShapeDtypeStruct((n, 2, stations, beams), jnp.bfloat16) for n in counts],
        ],
        compiler_params=pltpu.CompilerParams(vmem_limit_bytes=16 * MIB),
        cost_estimate=pl.CostEstimate(
            flops=200 * stations * beams, bytes_accessed=4 * (pairs + sum(counts)) * stations * beams, transcendentals=0
        ),
        name="turns",
    )(first, delays)


def beam_kernel(apart, step_ref, mid_ref, *refs):
    left, power = refs[-2:]
    r_refs, out_refs = refs[: -2 - apart], refs[-2 - apart : -2]
    lanes = r_refs[0].shape[3]
    _, _, beams = step_ref.shape
    half = lanes // 2
    width = 2 * LANES
    pairs = GROUP // 2
    j = pl.program_id(1)

    def lay(k, carry):
        both = [r[g, k].astype(jnp.float32) for r in r_refs for g in range(r.shape[0])]
        both = jnp.concatenate(both, 0).T
        left[k, 0] = both.astype(jnp.bfloat16)
        left[k, 1] = jnp.concatenate([both[half:], -both[:half]], 0).astype(jnp.bfloat16)
        return carry

    @pl.when(j == 0)
    def _():
        lax.fori_loop(0, GROUP, lay, 0, unroll=4)

    def one(k, cos, sin):
        out = jnp.dot(left[k, 0], cos.astype(jnp.bfloat16), preferred_element_type=jnp.float32)
        out = out + jnp.dot(left[k, 1], sin.astype(jnp.bfloat16), preferred_element_type=jnp.float32)
        energy = (out * out).reshape(2 * INTEG, lanes // (2 * INTEG), width)
        return jnp.sum(energy, 0) * (1.0 / INTEG)

    for b in range(beams // width):
        at = slice(b * width, (b + 1) * width)
        cm, sm = mid_ref[0, :, at], mid_ref[1, :, at]
        cj, sj = step_ref[0, :, at], step_ref[1, :, at]
        cc, ss, sc, cs = cm * cj, sm * sj, sm * cj, cm * sj
        power[pairs + j, :, at] = one(pairs + j, cc - ss, sc + cs)
        power[pairs - 1 - j, :, at] = one(pairs - 1 - j, cc + ss, sc - cs)
    mine = beams // out_refs[0].shape[0]
    whole, rest, part, share = packing(mine)

    def give(out_ref):
        for g in range(out_ref.shape[0]):
            own = power[:, :, g * mine : (g + 1) * mine]
            for t in range(whole):
                out_ref[g, t * GROUP : (t + 1) * GROUP] = own[:, :, t * LANES : (t + 1) * LANES].astype(jnp.bfloat16)
            if rest:
                tail = own[:, :, whole * LANES :]
                if part > rest:
                    tail = jnp.concatenate([tail, jnp.zeros((*tail.shape[:2], part - rest), tail.dtype)], 2)
                tail = jnp.concatenate([tail[m * share : (m + 1) * share] for m in range(LANES // part)], 2)
                out_ref[g, whole * GROUP :] = tail.astype(jnp.bfloat16)

    for n, out_ref in enumerate(out_refs):
        mine_now = (pl.program_id(0) == n) | (apart == 1)
        pl.when(mine_now & (j == pairs - 1))(functools.partial(give, out_ref))


def beams_of(steps, mids, received, owners, start, count, apart):
    pairs, _, stations, beams = steps.shape
    lanes = received[0][0].shape[3]
    powers = lanes // (2 * INTEG)
    whole, _, _, share = packing(beams // owners)
    rows = whole * GROUP + share
    held = count // apart
    return pl.pallas_call(
        functools.partial(beam_kernel, apart),
        grid=(count, pairs),
        in_specs=[
            pl.BlockSpec((None, 2, stations, beams), lambda i, j: (j, 0, 0, 0)),
            pl.BlockSpec((None, 2, stations, beams), lambda i, j: (i, 0, 0, 0)),
            *[
                pl.BlockSpec((r.shape[0], GROUP, r.shape[2], lanes), lambda i, j, at=at: (0, i + start - at, 0, 0))
                for r, at in received
            ],
        ],
        out_specs=[
            pl.BlockSpec((owners, None, rows, powers, LANES), lambda i, j: (0, i if apart == 1 else 0, 0, 0, 0))
        ] * apart,
        out_shape=[jax.ShapeDtypeStruct((owners, held, rows, powers, LANES), jnp.bfloat16)] * apart,
        scratch_shapes=[
            pltpu.VMEM((GROUP, 2, lanes, stations), jnp.bfloat16),
            pltpu.VMEM((GROUP, powers, beams), jnp.float32),
        ],
        compiler_params=pltpu.CompilerParams(vmem_limit_bytes=24 * MIB),
        cost_estimate=pl.CostEstimate(
            flops=8 * count * GROUP * beams * stations * lanes, bytes_accessed=4 * stations * beams, transcendentals=0
        ),
        name="beams",
    )(steps, mids, *[r for r, _ in received])


def tree_kernel(beams, moves_ref, own_ref, next_ref, *refs):

    out_ref, ping, pong = refs[-3:]
    sources, _, _, length, _ = own_ref.shape
    own_ref, next_ref = own_ref.at[:, 0], next_ref.at[:, 0]
    tiles, slots, depth, _ = ping.shape
    span = 2 * length
    whole, rest, part, share = packing(beams)
    for ref, at in ((own_ref, 0), (next_ref, length)):
        for s in range(sources):
            for t in range(whole):
                block = ref[s, t * GROUP : (t + 1) * GROUP].astype(jnp.float32)
                ping[t, s * GROUP : (s + 1) * GROUP, pl.ds(at, length), :] = block
            if rest:
                block = ref[s, whole * GROUP :].astype(jnp.float32)
                for m in range(LANES // part):
                    low = s * GROUP + m * share
                    moved = pltpu.roll(block, LANES - m * part, 2) if m else block
                    ping[whole, low : low + share, pl.ds(at, length), :] = moved
    src, dst = ping, pong
    for level in range(LEVELS):
        h = 2**level
        rows = span if level < LEVELS - 1 else length

        def tree(t, carry, src=src, dst=dst, h=h, rows=rows, level=level):
            start = t * GROUP
            for i in range(GROUP // 2):
                lead = start + i // h * 2 * h + i % h
                masks = []
                for r in range(2):
                    amount = jnp.broadcast_to(moves_ref[level, pl.ds(start + 2 * i + r, 1), :], (rows, LANES))
                    masks.append([amount == by for by in range(SHIFT_MOST)])
                for tile in range(tiles):
                    first = src[tile, lead, pl.ds(0, rows), :]
                    shifted = [src[tile, lead + h, pl.ds(by, rows), :] for by in range(SHIFT_MOST + 1)]
                    for r in range(2):
                        moved = shifted[SHIFT_MOST]
                        for by in range(SHIFT_MOST):
                            moved = jnp.where(masks[r][by], shifted[by], moved)
                        dst[tile, start + 2 * i + r, pl.ds(0, rows), :] = first + moved
            return carry

        lax.fori_loop(0, slots // GROUP, tree, 0)
        src, dst = dst, src
    for tile in range(tiles):
        flat = src.at[tile].reshape(slots * depth, LANES)
        here = min(LANES, beams - tile * LANES)
        for t in range(length):
            turned = (flat[pl.ds(t, slots, stride=depth), :] * 0.5**LEVELS).T
            out_ref[pl.ds(tile * LANES * length + t, here, stride=length), :] = turned[:here]


def dedisperse(moves, own, after, beams, first_slot, total, so_far):
    sources, groups, rows, length, _ = own.shape
    block = LANES // GROUP
    blocks = sources // block
    tiles = pl.cdiv(beams, LANES)
    depth = 2 * length + ROWS
    earlier = [] if so_far is None else [so_far]
    return pl.pallas_call(
        functools.partial(tree_kernel, beams),
        grid=(groups, blocks),
        in_specs=[
            pl.BlockSpec((LEVELS, LANES, LANES), lambda a, i: (0, first_slot // LANES + a * blocks + i, 0)),
            pl.BlockSpec((block, 1, rows, length, LANES), lambda a, i: (i, a, 0, 0, 0)),
            pl.BlockSpec((block, 1, rows, length, LANES), lambda a, i: (i, a, 0, 0, 0)),
            *[pl.BlockSpec(memory_space=pl.ANY) for _ in earlier],
        ],
        out_specs=pl.BlockSpec((beams * length, LANES), lambda a, i: (0, first_slot // LANES + a * blocks + i)),
        out_shape=jax.ShapeDtypeStruct((beams * length, total), jnp.float32),
        scratch_shapes=[pltpu.VMEM((tiles, LANES, depth, LANES), jnp.float32)] * 2,
        input_output_aliases={3: 0} if earlier else {},
        compiler_params=pltpu.CompilerParams(vmem_limit_bytes=16 * MIB),
        cost_estimate=pl.CostEstimate(
            flops=16 * beams * length * GROUP * sources * groups, bytes_accessed=10 * beams * length * GROUP * sources * groups, transcendentals=0
        ),
        name="dedisperse",
    )(moves, own, after, *earlier)


def swapped(x, owners):
    return lax.all_to_all(x.reshape(owners, -1, LANES), "grp", split_axis=0, concat_axis=0, tiled=True)


def local(voltages, filter_taps, delays, shifts):
    owners = lax.axis_size("grp")
    share = voltages.shape[1]
    groups = CHANNELS // (owners * GROUP)
    length = voltages.shape[2] // TRANSFORM // INTEG
    beams = delays.shape[1] // owners
    rim = voltages.shape[2] - (TAPS - 1) * TRANSFORM
    cuts = [0, ROWS, share] if share > ROWS else [0, share]
    early = [groups // 2, groups - groups // 2] if groups > 1 else [groups]
    moves = jnp.broadcast_to(shifts[:, :, None], (*shifts.shape, LANES))
    halos = []
    for n, (first, last) in enumerate(zip(cuts, cuts[1:])):
        halos.append(shift_along(voltages[:, first:last, rim:], "tm", 1))
    received = []
    for n, (first, last) in enumerate(zip(cuts, cuts[1:])):
        pieces = early if last == share else [groups]
        arrays = channelize(voltages, halos[n], filter_taps, owners, first, last, pieces)
        start = 0
        for many, array in zip(pieces, arrays):
            here = swapped(array, owners)
            here = here.reshape(owners, many * GROUP, last - first, LANES)
            if (last - first) % ROWS:
                here = jnp.transpose(here, (1, 0, 2, 3)).reshape(1, many * GROUP, -1, LANES)
            received.append((here, start, start + many))
            start += many
    by_owner = delays.reshape(owners, share, delays.shape[1])
    delays = jnp.concatenate([by_owner[:, a:b].reshape(-1, delays.shape[1]) for a, b in zip(cuts, cuts[1:])])
    mine = (lax.axis_index("grp") * GROUP).astype(jnp.int32).reshape(1)
    steps, *mids = turns(mine, delays, owners, early)
    out, start, n = None, 0, 0
    for call, many in enumerate(early):
        arrays = [(r, low) for r, low, high in received if low <= start and start + many <= high]
        apart = many if call else 1
        given = beams_of(steps, mids[call], arrays, owners, start, many, apart)
        for power in given:
            owned = swapped(power, owners).reshape(power.shape)
            after = shift_along(owned, "tm", -1)
            out = dedisperse(moves, owned, after, beams, start * owners * GROUP, CHANNELS, out)
            start += many // apart
            n += 1
    return jnp.transpose(out.reshape(beams, length, CHANNELS), (0, 2, 1))


def solution(mesh):
    placed = (P(None, "grp", "tm"), P(), P(), P())
    return jax.shard_map(local, mesh=mesh, in_specs=placed, out_specs=P("grp", None, "tm"), check_vma=False)
```
